32 devices in a mesh: rep: 2 (over x), grp: 4 (over z), tp: 4 (over y, core).
Axes of the slice: x: 2, y: 2, z: 4, core: 2. Of those that a mesh axis runs over, the one named last changes fastest.
Arguments:
- x_in: bfloat16 [4, 8, 128, 1280], P(None, ('rep', 'grp'), None, 'tp'), parts along dimension 1, may hold values from -6 to 6
- taps: bfloat16 [4, 8, 128, 6400], P(None, ('rep', 'grp'), None, 'tp'), parts along dimension 1, may hold values from -6 to 6
- ln_gain: float32 [1280], replicated, may hold values from 0.1 to 1.9
- ln_bias: float32 [1280], replicated, may hold values from -3 to 3
- w_up: bfloat16 [1280, 5120], P(None, 'tp'), may hold values from -0.15625 to 0.15625
- b_up: float32 [5120], P('tp'), may hold values from -3 to 3
- w_down: bfloat16 [5120, 1280], P('tp'), may hold values from -0.078125 to 0.078125
- b_down: float32 [1280], P('tp'), may hold values from -3 to 3
- kv_w_out: bfloat16 [1280, 2048], P('tp'), may hold values from -0.0625 to 0.0625
- kv_w_taps: bfloat16 [6400, 2048], P('tp'), may hold values from -0.09375 to 0.09375
- k_gain: float32 [128], replicated, may hold values from 1 to 2.5
- q_gain: float32 [128], replicated, may hold values from 1 to 2.5
- queries: bfloat16 [4096, 8192], P(('rep', 'grp'), 'tp'), parts along dimension 0, may hold values from -6 to 6
- tiles_per_request: int32 [16], P('rep'), parts along dimension 0, may hold values from 1 to 4, as said below
- owner: int32 [16], P('rep'), parts along dimension 0, may hold values from 0 to 3, as said below
- text_per_request: int32 [16], P('rep'), parts along dimension 0, may hold values from 64 to 256, as said below
Outputs:
- attended: bfloat16 [4096, 8192], P(('rep', 'grp'), 'tp'), parts along dimension 0
The draws below stay inside these ranges and needn't reach their ends.
There are 2 independent parts, one for each index of `rep`. The reference program is written for one: setup_inputs(seed, part) draws one part's arguments, and reference() takes and returns one part's arrays. A program takes and returns all parts, laid end to end along the dimension named above; an argument that names none is the same for every part. Nothing has to cross between parts.
Inputs may be any that keep to these rules, and one draw needn't show every extreme that they name: `owner`: each group owns exactly 2 requests. `tiles_per_request`: the tiles of all requests sum to 16; the tiles of one group's requests sum to at most 8, and some group has exactly 8. `text_per_request`: the text tokens of one group's requests sum to at most 512, and some group has exactly 512.
All inputs are finite; a program needn't handle non-finite values.
Results may differ from the reference program's by a relative error of at most 0.04.
Values may be sent and summed in bfloat16 or wider, within the bound.
A program may use at most 128 MiB of HBM per device.

```python
import math
import jax
import jax.numpy as jnp
from jax import lax

DV = 1280
MLPV = 5120
TAPS = 5
QH = 64
KVH = 8
HD = 128
TILE_ROWS = 128
TEXT_G = 512
TILES_ENC = 4
MAXT = 4
REQ_G = 2
FEAT = 7680
KVW = 2048
QW = 8192
TILES = 16
NREQ = 8
CAP = 8
N_GRP = 4
N_TP = 4


def owner_table(key):
    shuffled = jax.random.permutation(jax.random.fold_in(key, 101), NREQ)
    return (shuffled // REQ_G).astype(jnp.int32)


def chosen_group(key, salt):
    return jax.random.randint(jax.random.fold_in(key, salt), (), 0, N_GRP).astype(jnp.int32)


def draw_owner(key, part):
    return owner_table(key)


def draw_tiles_per_request(key, part):
    owners = owner_table(key)
    forced = owners == chosen_group(key, 202)
    extra_total = TILES - CAP - (NREQ - REQ_G)
    priority = jax.random.randint(jax.random.fold_in(key, 303), (max(extra_total, 1), NREQ), 0, 1 << 20)
    request_ids = jnp.arange(NREQ, dtype=jnp.int32)

    def add_one(step_index, extra):
        eligible = jnp.logical_not(forced) & (extra < MAXT - 1)
        ranked = jnp.where(eligible, priority[step_index], -1)
        picked = jnp.argmax(ranked).astype(jnp.int32)
        return extra + (request_ids == picked).astype(jnp.int32)
    extra = lax.fori_loop(0, extra_total, add_one, jnp.zeros((NREQ,), jnp.int32))
    return jnp.where(forced, MAXT, 1 + extra).astype(jnp.int32)


def draw_text_per_request(key, part):
    owners = owner_table(key)
    forced = owners == chosen_group(key, 404)
    base_counts = jax.random.randint(jax.random.fold_in(key, 505), (NREQ,), TEXT_G // 8, TEXT_G // 2 + 1)
    return jnp.where(forced, TEXT_G // 2, base_counts).astype(jnp.int32)


def with_spikes(values, rng, source, target, shards_of, factor):
    def block_of(dim):
        return (jnp.arange(values.shape[dim]) // (values.shape[dim] // shards_of)).reshape((-1,) + (1,) * (values.ndim - 1 - dim))

    near = jax.random.permutation(rng, shards_of)[block_of(target)]
    other_side = (block_of(target) + shards_of // 2) % shards_of
    return jnp.where((block_of(source) == near) | (block_of(source) == other_side), factor * values, values)


def steps_of(key, shape, split, least, high):
    def one(dim, parts):
        steps = jax.random.uniform(jax.random.fold_in(jax.random.fold_in(key, 6), dim), (parts,), jnp.float32, least / len(split), high / len(split))
        return jnp.repeat(jnp.exp(steps), shape[dim] // parts).reshape((-1,) + (1,) * (len(shape) - dim - 1))

    loudness = one(*split[0])
    for cut in split[1:]:
        loudness = loudness * one(*cut)
    return loudness


def gaussian(rng, shape, deviation, limit, split=(), kind=jnp.bfloat16):
    values = deviation * jax.random.normal(rng, shape, jnp.float32)
    if split:
        values = values * steps_of(rng, shape, split, -0.22, 0.18)
    return jnp.clip(values, -limit, limit).astype(kind)


def bell_draw_with(rng, dims, width, limit, shards, heavy, kind=jnp.bfloat16):
    values = width * jax.random.normal(rng, dims, jnp.float32)
    if shards:
        values = values * steps_of(rng, dims, shards, -0.22, 0.18)
    return jnp.clip(with_spikes(values, jax.random.fold_in(rng, 3), *heavy), -limit, limit).astype(kind)


def setup_inputs(seed: int = 0, part: int = 0) -> dict:
    keys = jax.random.split(jax.random.key(seed), 17)
    part_splits = jax.random.split(jax.random.fold_in(keys[16], part), 17)
    return {
        "x_in": gaussian(part_splits[0], (TILES_ENC, N_GRP, TILE_ROWS, DV), 1.0, 6.0, ((1, 4), (3, 4))),
        "taps": gaussian(part_splits[1], (TILES_ENC, N_GRP, TILE_ROWS, DV * TAPS), 1.0, 6.0, ((1, 4), (3, 4))),
        "ln_gain": jnp.clip(1.0 + 0.18 * jax.random.normal(keys[2], (DV,), jnp.float32), 0.1, 1.9),
        "ln_bias": gaussian(keys[3], (DV,), 0.5, 3.0, (), jnp.float32),
        "w_up": gaussian(keys[4], (DV, MLPV), DV ** -0.5, 0.15625, ((1, 4),)),
        "b_up": gaussian(keys[5], (MLPV,), 0.5, 3.0, ((0, 4),), jnp.float32),
        "w_down": gaussian(keys[6], (MLPV, DV), MLPV ** -0.5, 0.078125, ((0, 4),)),
        "b_down": gaussian(keys[7], (DV,), 0.5, 3.0, ((0, 4),), jnp.float32),
        "kv_w_out": gaussian(keys[8], (DV, KVW), FEAT ** -0.5, 0.0625, ((0, 4),)),
        "kv_w_taps": bell_draw_with(keys[9], (DV * TAPS, KVW), FEAT ** -0.5, 0.09375, ((0, 4),), (0, 1, 4, 2.0)),
        "k_gain": jnp.clip(jnp.exp(jax.random.uniform(keys[10], (HD,), jnp.float32, math.log(1.0), math.log(2.5))), 1.0, 2.5),
        "q_gain": jnp.clip(jnp.exp(jax.random.uniform(keys[11], (HD,), jnp.float32, math.log(1.0), math.log(2.5))), 1.0, 2.5),
        "queries": gaussian(part_splits[12], (N_GRP * TEXT_G, QW), 1.0, 6.0, ((0, 4), (1, 4))),
        "tiles_per_request": draw_tiles_per_request(jax.random.fold_in(jax.random.fold_in(keys[16], part), 71), part),
        "owner": draw_owner(jax.random.fold_in(jax.random.fold_in(keys[16], part), 71), part),
        "text_per_request": draw_text_per_request(jax.random.fold_in(jax.random.fold_in(keys[16], part), 71), part),
    }


epsilon = 1e-05

def layer_norm(row_block, ln_gain, ln_bias):
    values = row_block.astype(jnp.float32)
    average = lax.optimization_barrier(jnp.mean(values, axis=-1, keepdims=True))
    centered = values - average
    variance = lax.optimization_barrier(jnp.mean(centered * centered, axis=-1, keepdims=True))
    return (centered * lax.rsqrt(variance + epsilon) * ln_gain + ln_bias).astype(jnp.bfloat16)

def head_norm(values, head_gain):
    square = lax.optimization_barrier(jnp.mean(values * values, axis=-1, keepdims=True))
    return values * lax.rsqrt(square + epsilon) * head_gain

def group_layout(tiles_per_request, owner, text_per_request, group_count):
    request_count = owner.shape[0]
    request_ids = jnp.arange(request_count, dtype=jnp.int32)
    group_ids = jnp.arange(group_count, dtype=jnp.int32)
    member = owner[None, :] == group_ids[:, None]
    first_req = lax.optimization_barrier(jnp.min(jnp.where(member, request_ids[None, :], request_count), axis=1))
    second_req = lax.optimization_barrier(jnp.max(jnp.where(member, request_ids[None, :], -1), axis=1))
    pick_first = request_ids[None, :] == first_req[:, None]
    pick_second = request_ids[None, :] == second_req[:, None]
    tiles_first = lax.optimization_barrier(jnp.sum(jnp.where(pick_first, tiles_per_request[None, :], 0), axis=1)).astype(jnp.int32)
    tiles_second = lax.optimization_barrier(jnp.sum(jnp.where(pick_second, tiles_per_request[None, :], 0), axis=1)).astype(jnp.int32)
    text_first = lax.optimization_barrier(jnp.sum(jnp.where(pick_first, text_per_request[None, :], 0), axis=1)).astype(jnp.int32)
    text_second = lax.optimization_barrier(jnp.sum(jnp.where(pick_second, text_per_request[None, :], 0), axis=1)).astype(jnp.int32)
    tiles_both = (tiles_first + tiles_second).astype(jnp.int32)
    text_both = (text_first + text_second).astype(jnp.int32)
    offsets = (jnp.cumsum(tiles_both) - tiles_both).astype(jnp.int32)
    return (tiles_first, tiles_both, offsets, text_first, text_both)

def slot_label(position, first_count, both_count):
    return jnp.where(position < first_count, 0, jnp.where(position < both_count, 1, -1)).astype(jnp.int32)

def reference(x_in, taps, ln_gain, ln_bias, w_up, b_up, w_down, b_down, kv_w_out, kv_w_taps, k_gain, q_gain, queries, tiles_per_request, owner, text_per_request):
    token_count = TILES * TILE_ROWS
    token_rows = x_in.reshape(token_count, DV)
    normed = layer_norm(token_rows, ln_gain, ln_bias)
    hidden = jax.nn.gelu(jnp.dot(normed, w_up, preferred_element_type=jnp.float32) + b_up, approximate=False).astype(jnp.bfloat16)
    encoded = (token_rows.astype(jnp.float32) + jnp.dot(hidden, w_down, preferred_element_type=jnp.float32) + b_down).astype(jnp.bfloat16)
    tap_rows = taps.reshape(token_count, DV * TAPS)
    out_block = DV // N_TP
    tap_block = DV * TAPS // N_TP
    kv_total = jnp.zeros((token_count, KVW), jnp.float32)
    for block_index in range(N_TP):
        part_out = jnp.dot(encoded[:, block_index * out_block:(block_index + 1) * out_block], kv_w_out[block_index * out_block:(block_index + 1) * out_block], preferred_element_type=jnp.float32)
        part_tap = jnp.dot(tap_rows[:, block_index * tap_block:(block_index + 1) * tap_block], kv_w_taps[block_index * tap_block:(block_index + 1) * tap_block], preferred_element_type=jnp.float32)
        rounded = lax.optimization_barrier((part_out + part_tap).astype(jnp.bfloat16))
        kv_total = kv_total + rounded.astype(jnp.float32)
    kv_total = kv_total.reshape(TILES, TILE_ROWS, KVH, 2, HD)
    key_rows = head_norm(kv_total[:, :, :, 0, :], k_gain).astype(jnp.bfloat16)
    value_rows = kv_total[:, :, :, 1, :].astype(jnp.bfloat16)
    tiles_first, tiles_both, offsets, text_first, text_both = group_layout(tiles_per_request, owner, text_per_request, N_GRP)
    group_size = QH // KVH
    query_view = queries.reshape(N_GRP, TEXT_G, KVH, group_size, HD).astype(jnp.float32)
    query_rows = head_norm(query_view, q_gain).astype(jnp.bfloat16)
    slot_ids = jnp.arange(CAP, dtype=jnp.int32)
    text_ids = jnp.arange(TEXT_G, dtype=jnp.int32)
    scale = 1.0 / math_sqrt(HD)

    def per_group(item):
        query_group, first_count, both_count, offset, text_one, text_two = item
        tile_index = jnp.clip(offset + slot_ids, 0, TILES - 1).astype(jnp.int32)
        key_group = jnp.take(key_rows, tile_index, axis=0).reshape(CAP * TILE_ROWS, KVH, HD)
        value_group = jnp.take(value_rows, tile_index, axis=0).reshape(CAP * TILE_ROWS, KVH, HD)
        key_label = jnp.repeat(slot_label(slot_ids, first_count, both_count), TILE_ROWS)
        text_label = slot_label(text_ids, text_one, text_two)
        allowed = (text_label[:, None] == key_label[None, :]) & (text_label[:, None] >= 0)
        live_rows = text_label >= 0

        def per_head(head_item):
            query_head, key_head, value_head = head_item
            scores = jnp.einsum('tgd,sd->tgs', query_head.astype(jnp.float32), key_head.astype(jnp.float32)) * scale
            weights = jnp.where(allowed[:, None, :], jnp.exp(scores), 0.0)
            total = lax.optimization_barrier(jnp.sum(weights, axis=-1, keepdims=True))
            total = jnp.where(live_rows[:, None, None], total, 1.0)
            probs = jnp.where(live_rows[:, None, None], weights / total, 0.0).astype(jnp.bfloat16)
            result = jnp.einsum('tgs,sd->tgd', probs.astype(jnp.float32), value_head.astype(jnp.float32))
            return result.astype(jnp.bfloat16)
        head_out = lax.map(per_head, (jnp.transpose(query_group, (1, 0, 2, 3)), jnp.transpose(key_group, (1, 0, 2)), jnp.transpose(value_group, (1, 0, 2))))
        return jnp.transpose(head_out, (1, 0, 2, 3)).reshape(TEXT_G, QH * HD)
    attended = lax.map(per_group, (query_rows, tiles_first, tiles_both, offsets, text_first, text_both))
    return attended.reshape(N_GRP * TEXT_G, QH * HD)

def math_sqrt(number):
    return float(number) ** 0.5
```

```python
import functools

import jax
import jax.numpy as jnp
from jax import lax
from jax.experimental import pallas as pl
from jax.experimental.pallas import tpu as pltpu
from jax.sharding import PartitionSpec as P

KVH = 8
HD = 128
MAXT = 4
REQ_G = 2

epsilon = 1e-05
MESH = pl.DeviceIdType.MESH
VMEM_BYTES = 60 * 1024 * 1024
LOG2E = 1.4426950408889634
F32 = jnp.float32
BF16 = jnp.bfloat16


def front_kernel(
    sizes,
    x_hbm,
    taps_hbm,
    gain_ref,
    bias_ref,
    wup_hbm,
    bup_ref,
    wdn_hbm,
    bdn_ref,
    wko_hbm,
    wkt_hbm,
    kgain_ref,
    out_hbm,
    xg,
    normed,
    hidden,
    taps,
    wup,
    wdn,
    wko,
    wkt,
    kvt,
    m_send,
    m_r1,
    m_s2,
    m_r2,
    k_send,
    k_r1,
    k_s2,
    k_r2,
    kvg,
    w_sem,
    x_ssem,
    x_rsem,
    xp_ssem,
    xp_rsem,
    l1_ssem,
    l1_rsem,
    l2_ssem,
    l2_rsem,
    z_ssem,
    z_rsem,
    o_sem,
):
    tp_n, grp_n, nch, rc, chan, width = sizes
    chips = tp_n // 2
    tp_i = lax.axis_index("tp")
    grp_i = lax.axis_index("grp")
    core = lax.rem(tp_i, 2)
    chip = tp_i // 2
    other = 1 - core
    partner = {"tp": chip * 2 + other}

    def peer(dy):
        return lax.rem(chip + dy, chips)

    def peer_id(dy):
        return {"tp": peer(dy) * 2 + core}

    loads = [
        pltpu.make_async_copy(src, dst, w_sem.at[i])
        for i, (src, dst) in enumerate(
            [
                (x_hbm, xg.at[tp_i]),
                (taps_hbm, taps),
                (wkt_hbm, wkt),
                (wup_hbm, wup),
                (wdn_hbm, wdn),
                (wko_hbm, wko),
            ]
        )
    ]
    for load in loads:
        load.start()

    barrier = pltpu.get_barrier_semaphore()
    pl.semaphore_signal(barrier, inc=1, device_id=partner, device_id_type=MESH)
    for dy in range(1, chips):
        pl.semaphore_signal(barrier, inc=1, device_id=peer_id(dy), device_id_type=MESH)

    @pl.when(grp_i > 0)
    def _():
        pl.semaphore_signal(barrier, inc=1, device_id={"grp": grp_i - 1}, device_id_type=MESH)

    @pl.when(grp_i < grp_n - 1)
    def _():
        pl.semaphore_signal(barrier, inc=1, device_id={"grp": grp_i + 1}, device_id_type=MESH)

    neighbours = jnp.where(grp_i > 0, 1, 0) + jnp.where(grp_i < grp_n - 1, 1, 0)
    pl.semaphore_wait(barrier, chips + neighbours)

    def rows(ch):
        return pl.ds(ch * rc, rc)

    def x_copy(ch, dy):
        return pltpu.make_async_remote_copy(
            src_ref=x_hbm.at[rows(ch)],
            dst_ref=xg.at[tp_i, rows(ch)],
            send_sem=x_ssem.at[ch, dy],
            recv_sem=x_rsem.at[ch, dy],
            device_id=peer_id(dy) if dy else partner,
            device_id_type=MESH,
        )

    def x_pass(ch, dy):
        slot = lax.rem(chip - dy + chips, chips) * 2 + core
        return pltpu.make_async_remote_copy(
            src_ref=xg.at[slot, rows(ch)],
            dst_ref=xg.at[slot, rows(ch)],
            send_sem=xp_ssem.at[ch, dy],
            recv_sem=xp_rsem.at[ch, dy],
            device_id=partner,
            device_id_type=MESH,
        )

    def x_forward(ch):
        for dy in range(1, chips):
            x_copy(ch, dy).wait_recv()
            x_pass(ch, dy).start()

    for ch in range(nch):
        for dy in list(range(1, chips)) + [0]:
            x_copy(ch, dy).start()

    kv_cols = kvt.shape[1]

    def tap_product(ch):
        step = min(512, kv_cols)

        def body(j, carry):
            cols = pl.ds(pl.multiple_of(j * step, step), step)
            kvt[rows(ch), cols] = jnp.dot(
                taps[rows(ch), :], wkt[:, cols], preferred_element_type=F32
            )
            return carry

        lax.fori_loop(0, kv_cols // step, body, 0)

    def up(ch):
        if ch == 0:
            loads[0].wait()
        x_copy(ch, 0).wait_recv()
        for dy in range(1, chips):
            x_pass(ch, dy).wait_recv()
        depth = tp_n * chan
        total = jnp.zeros((rc, 1), F32)
        for b in range(tp_n):
            total = total + jnp.sum(xg[b, rows(ch), :].astype(F32), axis=-1, keepdims=True)
        average = total / depth
        square = jnp.zeros((rc, 1), F32)
        for b in range(tp_n):
            centered = xg[b, rows(ch), :].astype(F32) - average
            square = square + jnp.sum(centered * centered, axis=-1, keepdims=True)
        factor = lax.rsqrt(square / depth + epsilon)
        for b in range(tp_n):
            centered = xg[b, rows(ch), :].astype(F32) - average
            normed[:, b * chan : (b + 1) * chan] = (
                centered * factor * gain_ref[b] + bias_ref[b]
            ).astype(BF16)
        if ch == 0:
            loads[3].wait()
        units = hidden.shape[1]
        step = 256 if units % 256 == 0 else units

        def body(j, carry):
            cols = pl.ds(pl.multiple_of(j * step, step), step) if step < units else slice(None)
            pre = jnp.dot(normed[...], wup[:, cols], preferred_element_type=F32) + bup_ref[:, cols]
            hidden[:, cols] = (0.5 * pre * (1.0 + lax.erf(pre * (0.5**0.5)))).astype(BF16)
            return carry

        lax.fori_loop(0, units // step, body, 0)

    def down(ch):
        if ch == 0:
            loads[4].wait()
        terms = jnp.dot(hidden[...], wdn[...], preferred_element_type=F32).astype(BF16)
        for t in range(tp_n):
            m_send[ch, t % 2, t // 2] = terms[:, t * chan : (t + 1) * chan]

    def l1(which, ch):
        send, r1 = (m_send, m_r1) if which == 0 else (k_send, k_r1)
        return pltpu.make_async_remote_copy(
            src_ref=send.at[ch, other],
            dst_ref=r1.at[ch],
            send_sem=l1_ssem.at[which, ch],
            recv_sem=l1_rsem.at[which, ch],
            device_id=partner,
            device_id_type=MESH,
        )

    def l2(which, ch, dy):
        s2, r2 = (m_s2, m_r2) if which == 0 else (k_s2, k_r2)
        return pltpu.make_async_remote_copy(
            src_ref=s2.at[ch, dy - 1],
            dst_ref=r2.at[ch, dy - 1],
            send_sem=l2_ssem.at[which, ch, dy - 1],
            recv_sem=l2_rsem.at[which, ch, dy - 1],
            device_id=peer_id(dy),
            device_id_type=MESH,
        )

    def level2(which, ch):
        send, r1, s2 = (m_send, m_r1, m_s2) if which == 0 else (k_send, k_r1, k_s2)
        l1(which, ch).wait_recv()
        for dy in range(1, chips):
            y = peer(dy)
            s2[ch, dy - 1] = (send[ch, core, y].astype(F32) + r1[ch, y].astype(F32)).astype(BF16)
            l2(which, ch, dy).start()

    def summed(which, ch):
        send, r1, r2 = (m_send, m_r1, m_r2) if which == 0 else (k_send, k_r1, k_r2)
        total = send[ch, core, chip].astype(F32) + r1[ch, chip].astype(F32)
        for dy in range(1, chips):
            l2(which, ch, dy).wait_recv()
            total = total + r2[ch, dy - 1].astype(F32)
        return total

    def project(ch):
        if ch == 0:
            loads[5].wait()
        encoded = (
            xg[tp_i, rows(ch), :].astype(F32) + summed(0, ch) + bdn_ref[...]
        ).astype(BF16)
        for t in range(tp_n):
            start = t * KVH // tp_n * (2 * HD)
            cols = slice(start, start + width)
            k_send[ch, t % 2, t // 2] = (
                jnp.dot(encoded, wko[:, cols], preferred_element_type=F32) + kvt[rows(ch), cols]
            ).astype(BF16)

    def finish(ch):
        total = summed(1, ch)
        for h in range(width // (2 * HD)):
            key = total[:, 2 * h * HD : (2 * h + 1) * HD]
            square = jnp.mean(key * key, axis=-1, keepdims=True)
            kvg[ch, grp_i, :, 2 * h * HD : (2 * h + 1) * HD] = (
                key * lax.rsqrt(square + epsilon) * kgain_ref[...]
            ).astype(BF16)
            kvg[ch, grp_i, :, (2 * h + 1) * HD : (2 * h + 2) * HD] = total[
                :, (2 * h + 1) * HD : (2 * h + 2) * HD
            ].astype(BF16)

    def z_copy(ch, way, k):
        block = grp_i - k if way == 0 else grp_i + k
        block = jnp.clip(block, 0, grp_n - 1)
        target = grp_i + 1 if way == 0 else grp_i - 1
        return pltpu.make_async_remote_copy(
            src_ref=kvg.at[ch, block],
            dst_ref=kvg.at[ch, block],
            send_sem=z_ssem.at[way, ch, k],
            recv_sem=z_rsem.at[way, ch, k],
            device_id={"grp": target},
            device_id_type=MESH,
        )

    def z_sends(way, k):
        if way == 0:
            return (grp_i - k >= 0) & (grp_i < grp_n - 1)
        return (grp_i + k <= grp_n - 1) & (grp_i > 0)

    def z_gets(way, k):
        return grp_i - k - 1 >= 0 if way == 0 else grp_i + k + 1 <= grp_n - 1

    def z_start(ch, k):
        for way in range(2):
            @pl.when(z_sends(way, k))
            def _(way=way):
                z_copy(ch, way, k).start()

    def out_copy(ch, block, i):
        return pltpu.make_async_copy(kvg.at[ch, block], out_hbm.at[ch, block], o_sem.at[ch, i])

    def z_recv(ch, k):
        for way in range(2):
            @pl.when(z_gets(way, k))
            def _(way=way):
                z_copy(ch, way, k).wait_recv()

    def z_hop(ch, k):
        z_recv(ch, k)
        if k + 1 < grp_n - 1:
            z_start(ch, k + 1)

    loads[1].wait()
    loads[2].wait()
    for ch in range(nch):
        tap_product(ch)
        x_forward(ch)

    up(0)
    down(0)
    l1(0, 0).start()
    for ch in range(1, nch):
        up(ch)
        level2(0, ch - 1)
        down(ch)
        l1(0, ch).start()
    for ch in range(nch):
        project(ch)
        l1(1, ch).start()
        if ch == 0:
            level2(0, nch - 1)
        level2(1, ch)
        if ch > 0:
            finish(ch - 1)
            z_start(ch - 1, 0)
    finish(nch - 1)
    z_start(nch - 1, 0)
    for k in range(grp_n - 1):
        for ch in range(nch):
            z_hop(ch, k)

    copies = [out_copy(ch, b, b) for ch in range(nch) for b in range(grp_n)]
    for c in copies:
        c.start()
    for ch in range(nch):
        for dy in range(chips):
            x_copy(ch, dy).wait_send()
        for dy in range(1, chips):
            x_pass(ch, dy).wait_send()
        for which in range(2):
            l1(which, ch).wait_send()
            for dy in range(1, chips):
                l2(which, ch, dy).wait_send()
        for k in range(grp_n - 1):
            for way in range(2):
                @pl.when(z_sends(way, k))
                def _(ch=ch, way=way, k=k):
                    z_copy(ch, way, k).wait_send()
    for c in copies:
        c.wait()


def attend_kernel(
    tiles_ref, owner_ref, text_ref, q_ref, qgain_ref, kv_hbm, out_ref, kbuf, vbuf, sem
):
    nch, grp_n, rc, width = kv_hbm.shape
    kv_heads = width // (2 * HD)
    step = pl.program_id(0)
    group = lax.axis_index("grp")
    offset = jnp.int32(0)
    tiles = [jnp.int32(0), jnp.int32(0)]
    texts = [jnp.int32(0), jnp.int32(0)]
    seen = jnp.int32(0)
    for r in range(owner_ref.shape[0]):
        own = owner_ref[r] == group
        offset = offset + jnp.where(owner_ref[r] < group, tiles_ref[r], 0)
        for i in range(REQ_G):
            here = own & (seen == i)
            tiles[i] = jnp.where(here, tiles_ref[r], tiles[i])
            texts[i] = jnp.where(here, text_ref[r], texts[i])
        seen = seen + own.astype(jnp.int32)
    slots = REQ_G * MAXT
    tile = kbuf.shape[1] // slots
    per_chunk = rc // tile

    def copies(j, h):
        index = jnp.clip(offset + j, 0, grp_n * nch * per_chunk - 1)
        place, block = index // grp_n, lax.rem(index, grp_n)
        chunk, inside = place // per_chunk, lax.rem(place, per_chunk)
        src = kv_hbm.at[chunk, block, pl.ds(pl.multiple_of(inside * tile, tile), tile)]
        dst = pl.ds(j * tile, tile)
        return (
            pltpu.make_async_copy(src.at[:, pl.ds(2 * h * HD, HD)], kbuf.at[h, dst], sem.at[0, h, j]),
            pltpu.make_async_copy(
                src.at[:, pl.ds((2 * h + 1) * HD, HD)], vbuf.at[h, dst], sem.at[1, h, j]
            ),
        )

    everything = [(j, h) for h in range(kv_heads) for j in range(slots)]

    @pl.when(step == 0)
    def _():
        for j, h in everything:
            for c in copies(j, h):
                c.start()
        for j, h in everything:
            for c in copies(j, h):
                c.wait()

    head = step // (pl.num_programs(0) // kv_heads)
    query = q_ref[...].astype(F32)
    square = jnp.mean(query * query, axis=-1, keepdims=True)
    factor = qgain_ref[...] * (LOG2E / float(HD) ** 0.5)
    query = (query * lax.rsqrt(square + epsilon) * factor).astype(BF16)
    text_rows = q_ref.shape[0]
    block = 128 if text_rows % 128 == 0 else text_rows
    window = min(MAXT, slots) * tile
    out_ref[...] = jnp.zeros_like(out_ref)
    for rb in range(text_rows // block):
        for i in range(REQ_G):
            low = jnp.int32(0) if i == 0 else texts[0]
            high = low + texts[i]
            first = jnp.int32(0) if i == 0 else tiles[0]

            @pl.when((low < (rb + 1) * block) & (high > rb * block))
            def _():
                here = pl.ds(pl.multiple_of(first * tile, tile), window)
                scores = lax.dot_general(
                    query[rb * block : (rb + 1) * block],
                    kbuf[head, here, :],
                    (((1,), (1,)), ((), ())),
                    preferred_element_type=F32,
                )
                column = lax.broadcasted_iota(jnp.int32, (1, window), 1)
                weights = jnp.where(column < tiles[i] * tile, jnp.exp2(scores), 0.0)
                total = jnp.sum(weights, axis=-1, keepdims=True)
                row = lax.broadcasted_iota(jnp.int32, (block, 1), 0) + rb * block
                inverse = jnp.where((row >= low) & (row < high), 1.0 / total, 0.0)
                probs = (weights * inverse).astype(BF16)
                result = jnp.dot(probs, vbuf[head, here, :], preferred_element_type=F32)
                out_ref[rb * block : (rb + 1) * block, :] += result.astype(BF16)


def local(
    x_in,
    taps,
    ln_gain,
    ln_bias,
    w_up,
    b_up,
    w_down,
    b_down,
    kv_w_out,
    kv_w_taps,
    k_gain,
    q_gain,
    queries,
    tiles_per_request,
    owner,
    text_per_request,
):
    grp_n = lax.axis_size("grp")
    tp_n = lax.axis_size("tp")
    chips = tp_n // 2
    tiles_local, _, tile, chan = x_in.shape
    n = tiles_local * tile
    nch = 2 if tiles_local % 2 == 0 else 1
    rc = n // nch
    depth, units = w_up.shape
    tap_share, kv_cols = kv_w_taps.shape
    width = max(1, KVH // tp_n) * 2 * HD
    any_spec = pl.BlockSpec(memory_space=pl.ANY)
    vmem_spec = pl.BlockSpec(memory_space=pltpu.VMEM)
    dma = pltpu.SemaphoreType.DMA
    gathered = pl.pallas_call(
        functools.partial(front_kernel, (tp_n, grp_n, nch, rc, chan, width)),
        name="front",
        out_shape=jax.ShapeDtypeStruct((nch, grp_n, rc, width), BF16),
        in_specs=[
            any_spec,
            any_spec,
            vmem_spec,
            vmem_spec,
            any_spec,
            vmem_spec,
            any_spec,
            vmem_spec,
            any_spec,
            any_spec,
            vmem_spec,
        ],
        out_specs=any_spec,
        scratch_shapes=[
            pltpu.VMEM((tp_n, n, chan), BF16),
            pltpu.VMEM((rc, depth), BF16),
            pltpu.VMEM((rc, units), BF16),
            pltpu.VMEM((n, tap_share), BF16),
            pltpu.VMEM(w_up.shape, BF16),
            pltpu.VMEM(w_down.shape, BF16),
            pltpu.VMEM(kv_w_out.shape, BF16),
            pltpu.VMEM(kv_w_taps.shape, BF16),
            pltpu.VMEM((n, kv_cols), F32),
            pltpu.VMEM((nch, 2, chips, rc, chan), BF16),
            pltpu.VMEM((nch, chips, rc, chan), BF16),
            pltpu.VMEM((nch, chips - 1, rc, chan), BF16),
            pltpu.VMEM((nch, chips - 1, rc, chan), BF16),
            pltpu.VMEM((nch, 2, chips, rc, width), BF16),
            pltpu.VMEM((nch, chips, rc, width), BF16),
            pltpu.VMEM((nch, chips - 1, rc, width), BF16),
            pltpu.VMEM((nch, chips - 1, rc, width), BF16),
            pltpu.VMEM((nch, grp_n, rc, width), BF16),
            dma((6,)),
            dma((nch, chips)),
            dma((nch, chips)),
            dma((nch, chips)),
            dma((nch, chips)),
            dma((2, nch)),
            dma((2, nch)),
            dma((2, nch, chips - 1)),
            dma((2, nch, chips - 1)),
            dma((2, nch, grp_n - 1)),
            dma((2, nch, grp_n - 1)),
            dma((nch, grp_n)),
        ],
        compiler_params=pltpu.CompilerParams(
            collective_id=0, has_side_effects=True, vmem_limit_bytes=VMEM_BYTES
        ),
    )(
        x_in.reshape(n, chan),
        taps.reshape(n, tap_share),
        ln_gain.reshape(tp_n, 1, chan),
        ln_bias.reshape(tp_n, 1, chan),
        w_up,
        b_up.reshape(1, units),
        w_down,
        b_down.reshape(1, chan),
        kv_w_out,
        kv_w_taps,
        k_gain.reshape(1, HD),
    )
    text_rows, query_width = queries.shape
    heads = query_width // HD
    kv_heads = width // (2 * HD)
    slots = REQ_G * MAXT
    return pl.pallas_call(
        functools.partial(attend_kernel),
        name="attend",
        out_shape=jax.ShapeDtypeStruct(queries.shape, BF16),
        grid_spec=pltpu.PrefetchScalarGridSpec(
            num_scalar_prefetch=3,
            grid=(heads,),
            in_specs=[
                pl.BlockSpec((text_rows, HD), lambda h, *_: (0, h)),
                pl.BlockSpec((1, HD), lambda h, *_: (0, 0)),
                any_spec,
            ],
            out_specs=pl.BlockSpec((text_rows, HD), lambda h, *_: (0, h)),
            scratch_shapes=[
                pltpu.VMEM((kv_heads, slots * tile, HD), BF16),
                pltpu.VMEM((kv_heads, slots * tile, HD), BF16),
                dma((2, kv_heads, slots)),
            ],
        ),
        compiler_params=pltpu.CompilerParams(vmem_limit_bytes=VMEM_BYTES // 2),
    )(tiles_per_request, owner, text_per_request, queries, q_gain.reshape(1, HD), gathered)


def solution(mesh):
    in_specs = (
        P(None, ("rep", "grp"), None, "tp"),
        P(None, ("rep", "grp"), None, "tp"),
        P(),
        P(),
        P(None, "tp"),
        P("tp"),
        P("tp", None),
        P("tp"),
        P("tp", None),
        P("tp", None),
        P(),
        P(),
        P(("rep", "grp"), "tp"),
        P("rep"),
        P("rep"),
        P("rep"),
    )
    out_specs = P(("rep", "grp"), "tp")
    return jax.shard_map(local, mesh=mesh, in_specs=in_specs, out_specs=out_specs, check_vma=False)
```

```python
import functools

import jax
import jax.numpy as jnp
from jax import lax
from jax.experimental import pallas as pl
from jax.experimental.pallas import tpu as pltpu
from jax.sharding import PartitionSpec as P

KVH = 8
HD = 128
MAXT = 4
REQ_G = 2

epsilon = 1e-05
MESH = pl.DeviceIdType.MESH
VMEM_BYTES = 60 * 1024 * 1024
LOG2E = 1.4426950408889634
VALUE_SCALE = 65536.0
F32 = jnp.float32
BF16 = jnp.bfloat16


def front_kernel(
    sizes,
    x_hbm,
    taps_hbm,
    gain_ref,
    bias_ref,
    wup_hbm,
    bup_ref,
    wdn_hbm,
    bdn_ref,
    wko_hbm,
    wkt_hbm,
    kgain_ref,
    out_hbm,
    xg,
    normed,
    hidden,
    taps,
    tap_rows,
    wup,
    wdn,
    wko,
    wkt,
    kvt,
    m_send,
    m_r1,
    m_s2,
    m_r2,
    k_send,
    k_r1,
    k_s2,
    k_r2,
    kvg,
    w_sem,
    x_ssem,
    x_rsem,
    xp_ssem,
    xp_rsem,
    l1_ssem,
    l1_rsem,
    l2_ssem,
    l2_rsem,
    z_ssem,
    z_rsem,
    o_sem,
):
    tp_n, grp_n, nch, rc, chan, width = sizes
    tiles_ch = xg.shape[0] // nch
    tile = xg.shape[3]
    chips = tp_n // 2
    tp_i = lax.axis_index("tp")
    grp_i = lax.axis_index("grp")
    core = lax.rem(tp_i, 2)
    chip = tp_i // 2
    other = 1 - core
    partner = {"tp": chip * 2 + other}

    def peer(dy):
        return lax.rem(chip + dy, chips)

    def peer_id(dy):
        return {"tp": peer(dy) * 2 + core}

    loads = [
        pltpu.make_async_copy(src, dst, w_sem.at[i])
        for i, (src, dst) in enumerate(
            [
                (x_hbm.at[:, 0], xg.at[:, tp_i]),
                (taps_hbm.at[:, 0], taps),
                (wkt_hbm, wkt),
                (wup_hbm, wup),
                (wdn_hbm, wdn),
                (wko_hbm, wko),
            ]
        )
    ]
    for load in loads:
        load.start()

    barrier = pltpu.get_barrier_semaphore()
    pl.semaphore_signal(barrier, inc=1, device_id=partner, device_id_type=MESH)
    for dy in range(1, chips):
        pl.semaphore_signal(barrier, inc=1, device_id=peer_id(dy), device_id_type=MESH)

    @pl.when(grp_i > 0)
    def _():
        pl.semaphore_signal(barrier, inc=1, device_id={"grp": grp_i - 1}, device_id_type=MESH)

    @pl.when(grp_i < grp_n - 1)
    def _():
        pl.semaphore_signal(barrier, inc=1, device_id={"grp": grp_i + 1}, device_id_type=MESH)

    neighbours = jnp.where(grp_i > 0, 1, 0) + jnp.where(grp_i < grp_n - 1, 1, 0)
    pl.semaphore_wait(barrier, chips + neighbours)

    def rows(ch):
        return pl.ds(ch * rc, rc)

    def tiles_of(ch):
        return pl.ds(ch * tiles_ch, tiles_ch)

    def own_rows(ch):
        turned = [xg[ch * tiles_ch + i, tp_i].T for i in range(tiles_ch)]
        return jnp.concatenate(turned, axis=0).astype(F32)

    def x_copy(ch, dy):
        return pltpu.make_async_remote_copy(
            src_ref=x_hbm.at[tiles_of(ch), 0],
            dst_ref=xg.at[tiles_of(ch), tp_i],
            send_sem=x_ssem.at[ch, dy],
            recv_sem=x_rsem.at[ch, dy],
            device_id=peer_id(dy) if dy else partner,
            device_id_type=MESH,
        )

    def x_pass(ch, dy):
        slot = lax.rem(chip - dy + chips, chips) * 2 + core
        return pltpu.make_async_remote_copy(
            src_ref=xg.at[tiles_of(ch), slot],
            dst_ref=xg.at[tiles_of(ch), slot],
            send_sem=xp_ssem.at[ch, dy],
            recv_sem=xp_rsem.at[ch, dy],
            device_id=partner,
            device_id_type=MESH,
        )

    def x_forward(ch):
        for dy in range(1, chips):
            x_copy(ch, dy).wait_recv()
            x_pass(ch, dy).start()

    for ch in range(nch):
        for dy in list(range(1, chips)) + [0]:
            x_copy(ch, dy).start()

    kv_cols = kvt.shape[1]

    def tap_product(ch):
        step = min(512, kv_cols)

        def body(j, carry):
            cols = pl.ds(pl.multiple_of(j * step, step), step)
            kvt[rows(ch), cols] = jnp.dot(
                tap_rows[rows(ch), :], wkt[:, cols], preferred_element_type=F32
            )
            return carry

        lax.fori_loop(0, kv_cols // step, body, 0)

    def up(ch):
        if ch == 0:
            loads[0].wait()
        x_copy(ch, 0).wait_recv()
        for dy in range(1, chips):
            x_pass(ch, dy).wait_recv()
        depth = tp_n * chan
        gain = gain_ref[...].reshape(1, depth)
        bias = bias_ref[...].reshape(1, depth)
        for i in range(tiles_ch):
            values = xg[ch * tiles_ch + i].reshape(depth, tile).astype(F32)
            average = jnp.mean(values, axis=0, keepdims=True)
            centered = values - average
            variance = jnp.mean(centered * centered, axis=0, keepdims=True)
            standard = (centered * lax.rsqrt(variance + epsilon)).T
            normed[i * tile : (i + 1) * tile, :] = (standard * gain + bias).astype(BF16)
        if ch == 0:
            loads[3].wait()
        units = hidden.shape[1]
        step = 256 if units % 256 == 0 else units

        def body(j, carry):
            cols = pl.ds(pl.multiple_of(j * step, step), step) if step < units else slice(None)
            pre = jnp.dot(normed[...], wup[:, cols], preferred_element_type=F32) + bup_ref[cols].reshape(1, step)
            hidden[:, cols] = (0.5 * pre * (1.0 + lax.erf(pre * (0.5**0.5)))).astype(BF16)
            return carry

        lax.fori_loop(0, units // step, body, 0)

    def down(ch):
        if ch == 0:
            loads[4].wait()
        terms = jnp.dot(hidden[...], wdn[...], preferred_element_type=F32).astype(BF16)
        for t in range(tp_n):
            m_send[ch, t % 2, t // 2] = terms[:, t * chan : (t + 1) * chan]

    def l1(which, ch):
        send, r1 = (m_send, m_r1) if which == 0 else (k_send, k_r1)
        return pltpu.make_async_remote_copy(
            src_ref=send.at[ch, other],
            dst_ref=r1.at[ch],
            send_sem=l1_ssem.at[which, ch],
            recv_sem=l1_rsem.at[which, ch],
            device_id=partner,
            device_id_type=MESH,
        )

    def l2(which, ch, dy):
        s2, r2 = (m_s2, m_r2) if which == 0 else (k_s2, k_r2)
        return pltpu.make_async_remote_copy(
            src_ref=s2.at[ch, dy - 1],
            dst_ref=r2.at[ch, dy - 1],
            send_sem=l2_ssem.at[which, ch, dy - 1],
            recv_sem=l2_rsem.at[which, ch, dy - 1],
            device_id=peer_id(dy),
            device_id_type=MESH,
        )

    def level2(which, ch):
        send, r1, s2 = (m_send, m_r1, m_s2) if which == 0 else (k_send, k_r1, k_s2)
        l1(which, ch).wait_recv()
        for dy in range(1, chips):
            y = peer(dy)
            s2[ch, dy - 1] = (send[ch, core, y].astype(F32) + r1[ch, y].astype(F32)).astype(BF16)
            l2(which, ch, dy).start()

    def summed(which, ch):
        send, r1, r2 = (m_send, m_r1, m_r2) if which == 0 else (k_send, k_r1, k_r2)
        total = send[ch, core, chip].astype(F32) + r1[ch, chip].astype(F32)
        for dy in range(1, chips):
            l2(which, ch, dy).wait_recv()
            total = total + r2[ch, dy - 1].astype(F32)
        return total

    def project(ch):
        if ch == 0:
            loads[5].wait()
        encoded = (
            own_rows(ch) + summed(0, ch) + bdn_ref[...].reshape(1, chan)
        ).astype(BF16)
        for t in range(tp_n):
            start = t * KVH // tp_n * (2 * HD)
            cols = slice(start, start + width)
            k_send[ch, t % 2, t // 2] = (
                jnp.dot(encoded, wko[:, cols], preferred_element_type=F32) + kvt[rows(ch), cols]
            ).astype(BF16)

    def finish(ch):
        total = summed(1, ch)
        for h in range(width // (2 * HD)):
            key = total[:, 2 * h * HD : (2 * h + 1) * HD]
            square = jnp.mean(key * key, axis=-1, keepdims=True)
            kvg[ch, grp_i, :, 2 * h * HD : (2 * h + 1) * HD] = (
                key * lax.rsqrt(square + epsilon) * kgain_ref[...]
            ).astype(BF16)
            value = total[:, (2 * h + 1) * HD : (2 * h + 2) * HD]
            kvg[ch, grp_i, :, (2 * h + 1) * HD : (2 * h + 2) * HD] = (
                value * (1.0 / VALUE_SCALE)
            ).astype(BF16)

    def z_copy(ch, way, k):
        block = grp_i - k if way == 0 else grp_i + k
        block = jnp.clip(block, 0, grp_n - 1)
        target = grp_i + 1 if way == 0 else grp_i - 1
        return pltpu.make_async_remote_copy(
            src_ref=kvg.at[ch, block],
            dst_ref=kvg.at[ch, block],
            send_sem=z_ssem.at[way, ch, k],
            recv_sem=z_rsem.at[way, ch, k],
            device_id={"grp": target},
            device_id_type=MESH,
        )

    def z_sends(way, k):
        if way == 0:
            return (grp_i - k >= 0) & (grp_i < grp_n - 1)
        return (grp_i + k <= grp_n - 1) & (grp_i > 0)

    def z_gets(way, k):
        return grp_i - k - 1 >= 0 if way == 0 else grp_i + k + 1 <= grp_n - 1

    def z_start(ch, k):
        for way in range(2):
            @pl.when(z_sends(way, k))
            def _(way=way):
                z_copy(ch, way, k).start()

    def out_copy(ch, block, i):
        return pltpu.make_async_copy(kvg.at[ch, block], out_hbm.at[ch, block], o_sem.at[ch, i])

    def z_recv(ch, k):
        for way in range(2):
            @pl.when(z_gets(way, k))
            def _(way=way):
                z_copy(ch, way, k).wait_recv()

    def z_hop(ch, k):
        z_recv(ch, k)
        if k + 1 < grp_n - 1:
            z_start(ch, k + 1)

    loads[1].wait()
    for i in range(taps.shape[0]):
        tap_rows[i * tile : (i + 1) * tile, :] = taps[i].T
    loads[2].wait()
    for ch in range(nch):
        tap_product(ch)
        x_forward(ch)

    up(0)
    down(0)
    l1(0, 0).start()
    for ch in range(1, nch):
        up(ch)
        level2(0, ch - 1)
        down(ch)
        l1(0, ch).start()
    for ch in range(nch):
        project(ch)
        l1(1, ch).start()
        if ch == 0:
            level2(0, nch - 1)
        level2(1, ch)
        if ch > 0:
            finish(ch - 1)
            z_start(ch - 1, 0)
    finish(nch - 1)
    z_start(nch - 1, 0)
    for k in range(grp_n - 1):
        for ch in range(nch):
            z_hop(ch, k)

    copies = [out_copy(ch, b, b) for ch in range(nch) for b in range(grp_n)]
    for c in copies:
        c.start()
    for ch in range(nch):
        for dy in range(chips):
            x_copy(ch, dy).wait_send()
        for dy in range(1, chips):
            x_pass(ch, dy).wait_send()
        for which in range(2):
            l1(which, ch).wait_send()
            for dy in range(1, chips):
                l2(which, ch, dy).wait_send()
        for k in range(grp_n - 1):
            for way in range(2):
                @pl.when(z_sends(way, k))
                def _(ch=ch, way=way, k=k):
                    z_copy(ch, way, k).wait_send()
    for c in copies:
        c.wait()


def attend_kernel(
    tiles_ref, owner_ref, text_ref, q_ref, qgain_ref, kv_hbm, out_ref, kbuf, vbuf, vext, sem
):
    nch, grp_n, rc, width = kv_hbm.shape
    kv_heads = width // (2 * HD)
    requests, _, window, _ = kbuf.shape
    tile = window // MAXT
    head, rb = pl.program_id(0), pl.program_id(1)
    group = lax.axis_index("grp")
    offset = jnp.int32(0)
    tiles = [jnp.int32(0)] * requests
    texts = [jnp.int32(0)] * requests
    seen = jnp.int32(0)
    for r in range(owner_ref.shape[0]):
        own = owner_ref[r] == group
        offset = offset + jnp.where(owner_ref[r] < group, tiles_ref[r], 0)
        for i in range(requests):
            here = own & (seen == i)
            tiles[i] = jnp.where(here, tiles_ref[r], tiles[i])
            texts[i] = jnp.where(here, text_ref[r], texts[i])
        seen = seen + own.astype(jnp.int32)
    per_chunk = rc // tile

    def copies(i, h, j):
        first = jnp.int32(0) if i == 0 else tiles[0]
        index = jnp.clip(offset + first + j, 0, grp_n * nch * per_chunk - 1)
        place, block = index // grp_n, lax.rem(index, grp_n)
        chunk, inside = place // per_chunk, lax.rem(place, per_chunk)
        src = kv_hbm.at[chunk, block, pl.ds(pl.multiple_of(inside * tile, tile), tile)]
        dst = pl.ds(j * tile, tile)
        return (
            pltpu.make_async_copy(
                src.at[:, pl.ds(2 * h * HD, HD)], kbuf.at[i, h, dst], sem.at[0, i, h, j]
            ),
            pltpu.make_async_copy(
                src.at[:, pl.ds((2 * h + 1) * HD, HD)], vbuf.at[i, h, dst], sem.at[1, i, h, j]
            ),
        )

    @pl.when((head == 0) & (rb == 0))
    def _():
        for h in range(kv_heads):
            for i in range(requests):
                for j in range(MAXT):
                    for c in copies(i, h, j):
                        c.start()
        for h in range(kv_heads):
            for i in range(requests):
                for j in range(MAXT):
                    for c in copies(i, h, j):
                        c.wait()
                    rows = slice(j * tile, (j + 1) * tile)
                    live = j < tiles[i]
                    vext[i, h, rows, :HD] = jnp.where(live, vbuf[i, h, rows, :], 0).astype(BF16)
                    vext[i, h, rows, HD:] = jnp.where(live, jnp.ones((tile, HD), F32), 0.0).astype(BF16)

    block = q_ref.shape[0]
    per_head = q_ref.shape[1] // HD
    factor = qgain_ref[...] * (LOG2E / float(HD) ** 0.5)
    out_ref[...] = jnp.zeros_like(out_ref)
    row = lax.broadcasted_iota(jnp.int32, (block, 1), 0) + rb * block
    for i in range(requests):
        low = jnp.int32(0) if i == 0 else texts[0]
        high = low + texts[i]

        @pl.when((low < (rb + 1) * block) & (high > rb * block))
        def _():
            live = (row >= low) & (row < high)
            keys = kbuf[i, head]
            values = vext[i, head]
            for g in range(per_head):
                cols = slice(g * HD, (g + 1) * HD)
                query = q_ref[:, cols].astype(F32)
                square = jnp.mean(query * query, axis=-1, keepdims=True)
                query = (query * lax.rsqrt(square + epsilon) * factor).astype(BF16)
                scores = lax.dot_general(
                    query, keys, (((1,), (1,)), ((), ())), preferred_element_type=F32
                )
                weights = jnp.exp2(scores).astype(BF16)
                result = jnp.dot(weights, values, preferred_element_type=F32)
                shared = result[:, :HD] * (VALUE_SCALE / result[:, HD:])
                out_ref[:, cols] += jnp.where(live, shared, 0.0).astype(BF16)


def local(
    x_in,
    taps,
    ln_gain,
    ln_bias,
    w_up,
    b_up,
    w_down,
    b_down,
    kv_w_out,
    kv_w_taps,
    k_gain,
    q_gain,
    queries,
    tiles_per_request,
    owner,
    text_per_request,
):
    grp_n = lax.axis_size("grp")
    tp_n = lax.axis_size("tp")
    chips = tp_n // 2
    tiles_local, _, tile, chan = x_in.shape
    n = tiles_local * tile
    nch = 2 if tiles_local % 2 == 0 else 1
    rc = n // nch
    depth, units = w_up.shape
    tap_share, kv_cols = kv_w_taps.shape
    width = max(1, KVH // tp_n) * 2 * HD
    any_spec = pl.BlockSpec(memory_space=pl.ANY)
    vmem_spec = pl.BlockSpec(memory_space=pltpu.VMEM)
    dma = pltpu.SemaphoreType.DMA
    gathered = pl.pallas_call(
        functools.partial(front_kernel, (tp_n, grp_n, nch, rc, chan, width)),
        name="front",
        out_shape=jax.ShapeDtypeStruct((nch, grp_n, rc, width), BF16),
        in_specs=[
            any_spec,
            any_spec,
            vmem_spec,
            vmem_spec,
            any_spec,
            vmem_spec,
            any_spec,
            vmem_spec,
            any_spec,
            any_spec,
            vmem_spec,
        ],
        out_specs=any_spec,
        scratch_shapes=[
            pltpu.VMEM((tiles_local, tp_n, chan, tile), BF16),
            pltpu.VMEM((rc, depth), BF16),
            pltpu.VMEM((rc, units), BF16),
            pltpu.VMEM((tiles_local, tap_share, tile), BF16),
            pltpu.VMEM((n, tap_share), BF16),
            pltpu.VMEM(w_up.shape, BF16),
            pltpu.VMEM(w_down.shape, BF16),
            pltpu.VMEM(kv_w_out.shape, BF16),
            pltpu.VMEM(kv_w_taps.shape, BF16),
            pltpu.VMEM((n, kv_cols), F32),
            pltpu.VMEM((nch, 2, chips, rc, chan), BF16),
            pltpu.VMEM((nch, chips, rc, chan), BF16),
            pltpu.VMEM((nch, chips - 1, rc, chan), BF16),
            pltpu.VMEM((nch, chips - 1, rc, chan), BF16),
            pltpu.VMEM((nch, 2, chips, rc, width), BF16),
            pltpu.VMEM((nch, chips, rc, width), BF16),
            pltpu.VMEM((nch, chips - 1, rc, width), BF16),
            pltpu.VMEM((nch, chips - 1, rc, width), BF16),
            pltpu.VMEM((nch, grp_n, rc, width), BF16),
            dma((6,)),
            dma((nch, chips)),
            dma((nch, chips)),
            dma((nch, chips)),
            dma((nch, chips)),
            dma((2, nch)),
            dma((2, nch)),
            dma((2, nch, chips - 1)),
            dma((2, nch, chips - 1)),
            dma((2, nch, grp_n - 1)),
            dma((2, nch, grp_n - 1)),
            dma((nch, grp_n)),
        ],
        compiler_params=pltpu.CompilerParams(
            collective_id=0, has_side_effects=True, vmem_limit_bytes=VMEM_BYTES
        ),
    )(
        jnp.swapaxes(x_in, 2, 3),
        jnp.swapaxes(taps, 2, 3),
        ln_gain,
        ln_bias,
        w_up,
        b_up,
        w_down,
        b_down,
        kv_w_out,
        kv_w_taps,
        k_gain.reshape(1, HD),
    )
    text_rows, query_width = queries.shape
    heads = query_width // HD
    kv_heads = width // (2 * HD)
    block = 128 if text_rows % 128 == 0 else text_rows
    per_head = heads // kv_heads * HD
    spec = pl.BlockSpec((block, per_head), lambda h, r, *_: (r, h))
    return pl.pallas_call(
        attend_kernel,
        name="attend",
        out_shape=jax.ShapeDtypeStruct(queries.shape, BF16),
        grid_spec=pltpu.PrefetchScalarGridSpec(
            num_scalar_prefetch=3,
            grid=(kv_heads, text_rows // block),
            in_specs=[spec, pl.BlockSpec((1, HD), lambda h, r, *_: (0, 0)), any_spec],
            out_specs=spec,
            scratch_shapes=[
                pltpu.VMEM((REQ_G, kv_heads, MAXT * tile, HD), BF16),
                pltpu.VMEM((REQ_G, kv_heads, MAXT * tile, HD), BF16),
                pltpu.VMEM((REQ_G, kv_heads, MAXT * tile, 2 * HD), BF16),
                dma((2, REQ_G, kv_heads, MAXT)),
            ],
        ),
        compiler_params=pltpu.CompilerParams(vmem_limit_bytes=VMEM_BYTES),
    )(tiles_per_request, owner, text_per_request, queries, q_gain.reshape(1, HD), gathered)


def solution(mesh):
    in_specs = (
        P(None, ("rep", "grp"), None, "tp"),
        P(None, ("rep", "grp"), None, "tp"),
        P(),
        P(),
        P(None, "tp"),
        P("tp"),
        P("tp", None),
        P("tp"),
        P("tp", None),
        P("tp", None),
        P(),
        P(),
        P(("rep", "grp"), "tp"),
        P("rep"),
        P("rep"),
        P("rep"),
    )
    out_specs = P(("rep", "grp"), "tp")
    return jax.shard_map(local, mesh=mesh, in_specs=in_specs, out_specs=out_specs, check_vma=False)
```

```python
import functools

import jax
import jax.numpy as jnp
from jax import lax
from jax.experimental import pallas as pl
from jax.experimental.pallas import tpu as pltpu
from jax.sharding import PartitionSpec as P

KVH = 8
HD = 128
MAXT = 4
REQ_G = 2

epsilon = 1e-05
MESH = pl.DeviceIdType.MESH
VMEM_BYTES = 60 * 1024 * 1024
LOG2E = 1.4426950408889634
VALUE_SCALE = 65536.0
F32 = jnp.float32
BF16 = jnp.bfloat16


def front_kernel(
    sizes,
    x_hbm,
    taps_hbm,
    gain_ref,
    bias_ref,
    wup_hbm,
    bup_ref,
    wdn_hbm,
    bdn_ref,
    wko_hbm,
    wkt_hbm,
    kgain_ref,
    out_hbm,
    xg,
    normed,
    hidden,
    taps,
    tap_rows,
    wup,
    wdn,
    wko,
    wkt,
    kvt,
    m_send,
    m_r1,
    m_s2,
    m_r2,
    k_send,
    k_r1,
    k_s2,
    k_r2,
    kvg,
    w_sem,
    x_ssem,
    x_rsem,
    xp_ssem,
    xp_rsem,
    l1_ssem,
    l1_rsem,
    l2_ssem,
    l2_rsem,
    z_ssem,
    z_rsem,
    o_sem,
):
    tp_n, grp_n, nch, rc, chan, width = sizes
    tiles_ch = xg.shape[0] // nch
    tile = xg.shape[3]
    n_tiles = xg.shape[0]
    order = sorted(range(n_tiles), key=lambda t: abs(2 * t - n_tiles + 1))
    chunk_tiles = [order[c * tiles_ch : (c + 1) * tiles_ch] for c in range(nch)]
    total_tiles = n_tiles * grp_n
    chips = tp_n // 2
    tp_i = lax.axis_index("tp")
    grp_i = lax.axis_index("grp")
    core = lax.rem(tp_i, 2)
    chip = tp_i // 2
    other = 1 - core
    partner = {"tp": chip * 2 + other}

    def peer(dy):
        return lax.rem(chip + dy, chips)

    def peer_id(dy):
        return {"tp": peer(dy) * 2 + core}

    loads = [
        pltpu.make_async_copy(src, dst, w_sem.at[i])
        for i, (src, dst) in enumerate(
            [
                (x_hbm.at[:, 0], xg.at[:, tp_i]),
                (taps_hbm.at[:, 0], taps),
                (wkt_hbm, wkt),
                (wup_hbm, wup),
                (wdn_hbm, wdn),
                (wko_hbm, wko),
            ]
        )
    ]
    for load in loads:
        load.start()

    barrier = pltpu.get_barrier_semaphore()
    pl.semaphore_signal(barrier, inc=1, device_id=partner, device_id_type=MESH)
    for dy in range(1, chips):
        pl.semaphore_signal(barrier, inc=1, device_id=peer_id(dy), device_id_type=MESH)

    @pl.when(grp_i > 0)
    def _():
        pl.semaphore_signal(barrier, inc=1, device_id={"grp": grp_i - 1}, device_id_type=MESH)

    @pl.when(grp_i < grp_n - 1)
    def _():
        pl.semaphore_signal(barrier, inc=1, device_id={"grp": grp_i + 1}, device_id_type=MESH)

    neighbours = jnp.where(grp_i > 0, 1, 0) + jnp.where(grp_i < grp_n - 1, 1, 0)
    pl.semaphore_wait(barrier, chips + neighbours)

    def rows(ch):
        return pl.ds(ch * rc, rc)

    def own_rows(ch):
        turned = [xg[t, tp_i].T for t in chunk_tiles[ch]]
        return jnp.concatenate(turned, axis=0).astype(F32)

    def x_copy(t, dy):
        return pltpu.make_async_remote_copy(
            src_ref=x_hbm.at[t, 0],
            dst_ref=xg.at[t, tp_i],
            send_sem=x_ssem.at[t, dy],
            recv_sem=x_rsem.at[t, dy],
            device_id=peer_id(dy) if dy else partner,
            device_id_type=MESH,
        )

    def x_pass(t, dy):
        slot = lax.rem(chip - dy + chips, chips) * 2 + core
        return pltpu.make_async_remote_copy(
            src_ref=xg.at[t, slot],
            dst_ref=xg.at[t, slot],
            send_sem=xp_ssem.at[t, dy],
            recv_sem=xp_rsem.at[t, dy],
            device_id=partner,
            device_id_type=MESH,
        )

    def x_forward(ch):
        for t in chunk_tiles[ch]:
            for dy in range(1, chips):
                x_copy(t, dy).wait_recv()
                x_pass(t, dy).start()

    for t in order:
        for dy in list(range(1, chips)) + [0]:
            x_copy(t, dy).start()

    kv_cols = kvt.shape[1]

    def tap_product(ch):
        step = min(512, kv_cols)

        def body(j, carry):
            cols = pl.ds(pl.multiple_of(j * step, step), step)
            kvt[rows(ch), cols] = jnp.dot(
                tap_rows[rows(ch), :], wkt[:, cols], preferred_element_type=F32
            )
            return carry

        lax.fori_loop(0, kv_cols // step, body, 0)

    def up(ch):
        if ch == 0:
            loads[0].wait()
        for t in chunk_tiles[ch]:
            x_copy(t, 0).wait_recv()
            for dy in range(1, chips):
                x_pass(t, dy).wait_recv()
        depth = tp_n * chan
        gain = gain_ref[...].reshape(1, depth)
        bias = bias_ref[...].reshape(1, depth)
        for i, t in enumerate(chunk_tiles[ch]):
            values = xg[t].reshape(depth, tile).astype(F32)
            average = jnp.mean(values, axis=0, keepdims=True)
            centered = values - average
            variance = jnp.mean(centered * centered, axis=0, keepdims=True)
            standard = (centered * lax.rsqrt(variance + epsilon)).T
            normed[i * tile : (i + 1) * tile, :] = (standard * gain + bias).astype(BF16)
        if ch == 0:
            loads[3].wait()
        units = hidden.shape[1]
        step = 256 if units % 256 == 0 else units

        def body(j, carry):
            cols = pl.ds(pl.multiple_of(j * step, step), step) if step < units else slice(None)
            pre = jnp.dot(normed[...], wup[:, cols], preferred_element_type=F32) + bup_ref[cols].reshape(1, step)
            hidden[:, cols] = (0.5 * pre * (1.0 + lax.erf(pre * (0.5**0.5)))).astype(BF16)
            return carry

        lax.fori_loop(0, units // step, body, 0)

    def down(ch):
        if ch == 0:
            loads[4].wait()
        terms = jnp.dot(hidden[...], wdn[...], preferred_element_type=F32).astype(BF16)
        for t in range(tp_n):
            m_send[ch, t % 2, t // 2] = terms[:, t * chan : (t + 1) * chan]

    def l1(which, ch):
        send, r1 = (m_send, m_r1) if which == 0 else (k_send, k_r1)
        return pltpu.make_async_remote_copy(
            src_ref=send.at[ch, other],
            dst_ref=r1.at[ch],
            send_sem=l1_ssem.at[which, ch],
            recv_sem=l1_rsem.at[which, ch],
            device_id=partner,
            device_id_type=MESH,
        )

    def l2(which, ch, dy):
        s2, r2 = (m_s2, m_r2) if which == 0 else (k_s2, k_r2)
        return pltpu.make_async_remote_copy(
            src_ref=s2.at[ch, dy - 1],
            dst_ref=r2.at[ch, dy - 1],
            send_sem=l2_ssem.at[which, ch, dy - 1],
            recv_sem=l2_rsem.at[which, ch, dy - 1],
            device_id=peer_id(dy),
            device_id_type=MESH,
        )

    def level2(which, ch):
        send, r1, s2 = (m_send, m_r1, m_s2) if which == 0 else (k_send, k_r1, k_s2)
        l1(which, ch).wait_recv()
        for dy in range(1, chips):
            y = peer(dy)
            s2[ch, dy - 1] = (send[ch, core, y].astype(F32) + r1[ch, y].astype(F32)).astype(BF16)
            l2(which, ch, dy).start()

    def summed(which, ch):
        send, r1, r2 = (m_send, m_r1, m_r2) if which == 0 else (k_send, k_r1, k_r2)
        total = send[ch, core, chip].astype(F32) + r1[ch, chip].astype(F32)
        for dy in range(1, chips):
            l2(which, ch, dy).wait_recv()
            total = total + r2[ch, dy - 1].astype(F32)
        return total

    def project(ch):
        if ch == 0:
            loads[5].wait()
        encoded = (
            own_rows(ch) + summed(0, ch) + bdn_ref[...].reshape(1, chan)
        ).astype(BF16)
        for t in range(tp_n):
            start = t * KVH // tp_n * (2 * HD)
            cols = slice(start, start + width)
            k_send[ch, t % 2, t // 2] = (
                jnp.dot(encoded, wko[:, cols], preferred_element_type=F32) + kvt[rows(ch), cols]
            ).astype(BF16)

    def finish(ch):
        total = summed(1, ch)
        for h in range(width // (2 * HD)):
            key = total[:, 2 * h * HD : (2 * h + 1) * HD]
            square = jnp.mean(key * key, axis=-1, keepdims=True)
            key = (key * lax.rsqrt(square + epsilon) * kgain_ref[...]).astype(BF16)
            value = total[:, (2 * h + 1) * HD : (2 * h + 2) * HD]
            value = (value * (1.0 / VALUE_SCALE)).astype(BF16)
            for i, t in enumerate(chunk_tiles[ch]):
                part = slice(i * tile, (i + 1) * tile)
                kvg[t, grp_i, :, 2 * h * HD : (2 * h + 1) * HD] = key[part]
                kvg[t, grp_i, :, (2 * h + 1) * HD : (2 * h + 2) * HD] = value[part]

    def least(p):
        return jnp.maximum(REQ_G * p, total_tiles - REQ_G * MAXT * (grp_n - p))

    def most(p):
        return jnp.minimum(REQ_G * MAXT * (p + 1), total_tiles - REQ_G * (grp_n - 1 - p))

    def z_copy(t, way, k):
        block = grp_i - k if way == 0 else grp_i + k
        block = jnp.clip(block, 0, grp_n - 1)
        target = grp_i + 1 if way == 0 else grp_i - 1
        return pltpu.make_async_remote_copy(
            src_ref=kvg.at[t, block],
            dst_ref=kvg.at[t, block],
            send_sem=z_ssem.at[way, t, k],
            recv_sem=z_rsem.at[way, t, k],
            device_id={"grp": target},
            device_id_type=MESH,
        )

    def z_sends(t, way, k):
        if way == 0:
            tile_id = t * grp_n + grp_i - k
            return (grp_i - k >= 0) & (grp_i < grp_n - 1) & (tile_id >= least(grp_i + 1))
        tile_id = t * grp_n + grp_i + k
        return (grp_i + k <= grp_n - 1) & (grp_i > 0) & (tile_id < most(grp_i - 1))

    def z_gets(t, way, k):
        if way == 0:
            return (grp_i - k - 1 >= 0) & (t * grp_n + grp_i - k - 1 >= least(grp_i))
        return (grp_i + k + 1 <= grp_n - 1) & (t * grp_n + grp_i + k + 1 < most(grp_i))

    def z_start(t, k):
        for way in range(2):
            @pl.when(z_sends(t, way, k))
            def _(way=way):
                z_copy(t, way, k).start()

    def out_copy(t, block):
        return pltpu.make_async_copy(kvg.at[t, block], out_hbm.at[t, block], o_sem.at[t, block])

    def owned(t, block):
        tile_id = t * grp_n + block
        return (tile_id >= least(grp_i)) & (tile_id < most(grp_i))

    def z_hop(t, k):
        for way in range(2):
            @pl.when(z_gets(t, way, k))
            def _(way=way):
                z_copy(t, way, k).wait_recv()
            if k + 1 < grp_n - 1:
                @pl.when(z_sends(t, way, k + 1))
                def _(way=way):
                    z_copy(t, way, k + 1).start()

    loads[1].wait()
    for i, t in enumerate(order):
        tap_rows[i * tile : (i + 1) * tile, :] = taps[t].T
    loads[2].wait()
    ahead = min(2, nch)
    for ch in range(ahead):
        tap_product(ch)
        x_forward(ch)
    for step in range(nch + grp_n + 4):
        if step < nch:
            up(step)
        if 0 <= step - 1 < nch:
            level2(0, step - 1)
        if step < nch:
            down(step)
            l1(0, step).start()
        if ahead <= step + ahead < nch:
            x_forward(step + ahead)
        if 0 <= step - 3 < nch:
            level2(1, step - 3)
        if ahead <= step + ahead < nch:
            tap_product(step + ahead)
        if 0 <= step - 2 < nch:
            project(step - 2)
            l1(1, step - 2).start()
        if 0 <= step - 4 < nch:
            finish(step - 4)
            for t in chunk_tiles[step - 4]:
                z_start(t, 0)
        for k in range(grp_n - 1):
            if 0 <= step - 5 - k < nch:
                for t in chunk_tiles[step - 5 - k]:
                    z_hop(t, k)

    for t in range(n_tiles):
        for block in range(grp_n):
            @pl.when(owned(t, block))
            def _(t=t, block=block):
                out_copy(t, block).start()
    for t in range(n_tiles):
        for dy in range(chips):
            x_copy(t, dy).wait_send()
        for dy in range(1, chips):
            x_pass(t, dy).wait_send()
        for k in range(grp_n - 1):
            for way in range(2):
                @pl.when(z_sends(t, way, k))
                def _(t=t, way=way, k=k):
                    z_copy(t, way, k).wait_send()
    for ch in range(nch):
        for which in range(2):
            l1(which, ch).wait_send()
            for dy in range(1, chips):
                l2(which, ch, dy).wait_send()
    for t in range(n_tiles):
        for block in range(grp_n):
            @pl.when(owned(t, block))
            def _(t=t, block=block):
                out_copy(t, block).wait()


def attend_kernel(
    tiles_ref, owner_ref, text_ref, q_ref, qgain_ref, kv_hbm, out_ref, kbuf, vbuf, vext, sem
):
    _, grp_n, _, width = kv_hbm.shape
    kv_heads = width // (2 * HD)
    requests, _, window, _ = kbuf.shape
    tile = window // MAXT
    head, rb = pl.program_id(0), pl.program_id(1)
    group = lax.axis_index("grp")
    offset = jnp.int32(0)
    tiles = [jnp.int32(0)] * requests
    texts = [jnp.int32(0)] * requests
    seen = jnp.int32(0)
    for r in range(owner_ref.shape[0]):
        own = owner_ref[r] == group
        offset = offset + jnp.where(owner_ref[r] < group, tiles_ref[r], 0)
        for i in range(requests):
            here = own & (seen == i)
            tiles[i] = jnp.where(here, tiles_ref[r], tiles[i])
            texts[i] = jnp.where(here, text_ref[r], texts[i])
        seen = seen + own.astype(jnp.int32)

    def copies(i, h, j):
        first = jnp.int32(0) if i == 0 else tiles[0]
        index = offset + first + jnp.where(j < tiles[i], j, 0)
        src = kv_hbm.at[index // grp_n, lax.rem(index, grp_n)]
        dst = pl.ds(j * tile, tile)
        return (
            pltpu.make_async_copy(
                src.at[:, pl.ds(2 * h * HD, HD)], kbuf.at[i, h, dst], sem.at[0, i, h, j]
            ),
            pltpu.make_async_copy(
                src.at[:, pl.ds((2 * h + 1) * HD, HD)], vbuf.at[i, h, dst], sem.at[1, i, h, j]
            ),
        )

    @pl.when((head == 0) & (rb == 0))
    def _():
        for h in range(kv_heads):
            for i in range(requests):
                for j in range(MAXT):
                    for c in copies(i, h, j):
                        c.start()
        for h in range(kv_heads):
            for i in range(requests):
                for j in range(MAXT):
                    for c in copies(i, h, j):
                        c.wait()
                    rows = slice(j * tile, (j + 1) * tile)
                    live = j < tiles[i]
                    vext[i, h, rows, :HD] = jnp.where(live, vbuf[i, h, rows, :], 0).astype(BF16)
                    vext[i, h, rows, HD:] = jnp.where(live, jnp.ones((tile, HD), F32), 0.0).astype(BF16)

    block = q_ref.shape[0]
    per_head = q_ref.shape[1] // HD
    factor = qgain_ref[...] * (LOG2E / float(HD) ** 0.5)
    out_ref[...] = jnp.zeros_like(out_ref)
    row = lax.broadcasted_iota(jnp.int32, (block, 1), 0) + rb * block
    for i in range(requests):
        low = jnp.int32(0) if i == 0 else texts[0]
        high = low + texts[i]

        @pl.when((low < (rb + 1) * block) & (high > rb * block))
        def _():
            live = (row >= low) & (row < high)
            keys = kbuf[i, head]
            values = vext[i, head]
            for g in range(per_head):
                cols = slice(g * HD, (g + 1) * HD)
                query = q_ref[:, cols].astype(F32)
                square = jnp.mean(query * query, axis=-1, keepdims=True)
                query = (query * lax.rsqrt(square + epsilon) * factor).astype(BF16)
                scores = lax.dot_general(
                    query, keys, (((1,), (1,)), ((), ())), preferred_element_type=F32
                )
                weights = jnp.exp2(scores).astype(BF16)
                result = jnp.dot(weights, values, preferred_element_type=F32)
                shared = result[:, :HD] * (VALUE_SCALE / result[:, HD:])
                out_ref[:, cols] += jnp.where(live, shared, 0.0).astype(BF16)


def local(
    x_in,
    taps,
    ln_gain,
    ln_bias,
    w_up,
    b_up,
    w_down,
    b_down,
    kv_w_out,
    kv_w_taps,
    k_gain,
    q_gain,
    queries,
    tiles_per_request,
    owner,
    text_per_request,
):
    grp_n = lax.axis_size("grp")
    tp_n = lax.axis_size("tp")
    chips = tp_n // 2
    tiles_local, _, tile, chan = x_in.shape
    n = tiles_local * tile
    nch = tiles_local
    rc = n // nch
    depth, units = w_up.shape
    tap_share, kv_cols = kv_w_taps.shape
    width = max(1, KVH // tp_n) * 2 * HD
    any_spec = pl.BlockSpec(memory_space=pl.ANY)
    vmem_spec = pl.BlockSpec(memory_space=pltpu.VMEM)
    dma = pltpu.SemaphoreType.DMA
    gathered = pl.pallas_call(
        functools.partial(front_kernel, (tp_n, grp_n, nch, rc, chan, width)),
        name="front",
        out_shape=jax.ShapeDtypeStruct((tiles_local, grp_n, tile, width), BF16),
        in_specs=[
            any_spec,
            any_spec,
            vmem_spec,
            vmem_spec,
            any_spec,
            vmem_spec,
            any_spec,
            vmem_spec,
            any_spec,
            any_spec,
            vmem_spec,
        ],
        out_specs=any_spec,
        scratch_shapes=[
            pltpu.VMEM((tiles_local, tp_n, chan, tile), BF16),
            pltpu.VMEM((rc, depth), BF16),
            pltpu.VMEM((rc, units), BF16),
            pltpu.VMEM((tiles_local, tap_share, tile), BF16),
            pltpu.VMEM((n, tap_share), BF16),
            pltpu.VMEM(w_up.shape, BF16),
            pltpu.VMEM(w_down.shape, BF16),
            pltpu.VMEM(kv_w_out.shape, BF16),
            pltpu.VMEM(kv_w_taps.shape, BF16),
            pltpu.VMEM((n, kv_cols), F32),
            pltpu.VMEM((nch, 2, chips, rc, chan), BF16),
            pltpu.VMEM((nch, chips, rc, chan), BF16),
            pltpu.VMEM((nch, chips - 1, rc, chan), BF16),
            pltpu.VMEM((nch, chips - 1, rc, chan), BF16),
            pltpu.VMEM((nch, 2, chips, rc, width), BF16),
            pltpu.VMEM((nch, chips, rc, width), BF16),
            pltpu.VMEM((nch, chips - 1, rc, width), BF16),
            pltpu.VMEM((nch, chips - 1, rc, width), BF16),
            pltpu.VMEM((tiles_local, grp_n, tile, width), BF16),
            dma((6,)),
            dma((tiles_local, chips)),
            dma((tiles_local, chips)),
            dma((tiles_local, chips)),
            dma((tiles_local, chips)),
            dma((2, nch)),
            dma((2, nch)),
            dma((2, nch, chips - 1)),
            dma((2, nch, chips - 1)),
            dma((2, tiles_local, grp_n - 1)),
            dma((2, tiles_local, grp_n - 1)),
            dma((tiles_local, grp_n)),
        ],
        compiler_params=pltpu.CompilerParams(
            collective_id=0, has_side_effects=True, vmem_limit_bytes=VMEM_BYTES
        ),
    )(
        jnp.swapaxes(x_in, 2, 3),
        jnp.swapaxes(taps, 2, 3),
        ln_gain,
        ln_bias,
        w_up,
        b_up,
        w_down,
        b_down,
        kv_w_out,
        kv_w_taps,
        k_gain.reshape(1, HD),
    )
    text_rows, query_width = queries.shape
    heads = query_width // HD
    kv_heads = width // (2 * HD)
    block = 128 if text_rows % 128 == 0 else text_rows
    per_head = heads // kv_heads * HD
    spec = pl.BlockSpec((block, per_head), lambda h, r, *_: (r, h))
    return pl.pallas_call(
        attend_kernel,
        name="attend",
        out_shape=jax.ShapeDtypeStruct(queries.shape, BF16),
        grid_spec=pltpu.PrefetchScalarGridSpec(
            num_scalar_prefetch=3,
            grid=(kv_heads, text_rows // block),
            in_specs=[spec, pl.BlockSpec((1, HD), lambda h, r, *_: (0, 0)), any_spec],
            out_specs=spec,
            scratch_shapes=[
                pltpu.VMEM((REQ_G, kv_heads, MAXT * tile, HD), BF16),
                pltpu.VMEM((REQ_G, kv_heads, MAXT * tile, HD), BF16),
                pltpu.VMEM((REQ_G, kv_heads, MAXT * tile, 2 * HD), BF16),
                dma((2, REQ_G, kv_heads, MAXT)),
            ],
        ),
        compiler_params=pltpu.CompilerParams(vmem_limit_bytes=VMEM_BYTES),
    )(tiles_per_request, owner, text_per_request, queries, q_gain.reshape(1, HD), gathered)


def solution(mesh):
    in_specs = (
        P(None, ("rep", "grp"), None, "tp"),
        P(None, ("rep", "grp"), None, "tp"),
        P(),
        P(),
        P(None, "tp"),
        P("tp"),
        P("tp", None),
        P("tp"),
        P("tp", None),
        P("tp", None),
        P(),
        P(),
        P(("rep", "grp"), "tp"),
        P("rep"),
        P("rep"),
        P("rep"),
    )
    out_specs = P(("rep", "grp"), "tp")
    return jax.shard_map(local, mesh=mesh, in_specs=in_specs, out_specs=out_specs, check_vma=False)
```

```python
import functools

import jax
import jax.numpy as jnp
from jax import lax
from jax.experimental import pallas as pl
from jax.experimental.pallas import tpu as pltpu
from jax.sharding import PartitionSpec as P

KVH = 8
HD = 128
MAXT = 4
REQ_G = 2

epsilon = 1e-05
MESH = pl.DeviceIdType.MESH
VMEM_BYTES = 60 * 1024 * 1024
LOG2E = 1.4426950408889634
VALUE_SCALE = 65536.0
F32 = jnp.float32
BF16 = jnp.bfloat16


def front_kernel(
    sizes,
    x_hbm,
    taps_hbm,
    gain_ref,
    bias_ref,
    wup_hbm,
    bup_ref,
    wdn_hbm,
    bdn_ref,
    wko_hbm,
    wkt_hbm,
    kgain_ref,
    out_hbm,
    xg,
    normed,
    hidden,
    taps,
    tap_rows,
    wup,
    wdn,
    wko,
    wkt,
    kvt,
    m_send,
    m_r1,
    m_s2,
    m_r2,
    k_send,
    k_r1,
    k_s2,
    k_r2,
    kvg,
    w_sem,
    x_ssem,
    x_rsem,
    xp_ssem,
    xp_rsem,
    l1_ssem,
    l1_rsem,
    l2_ssem,
    l2_rsem,
    z_ssem,
    z_rsem,
    o_sem,
):
    tp_n, grp_n, nch, rc, chan, width = sizes
    tiles_ch = xg.shape[0] // nch
    tile = xg.shape[3]
    n_tiles = xg.shape[0]
    order = sorted(range(n_tiles), key=lambda t: abs(2 * t - n_tiles + 1))
    chunk_tiles = [order[c * tiles_ch : (c + 1) * tiles_ch] for c in range(nch)]
    total_tiles = n_tiles * grp_n
    chips = tp_n // 2
    tp_i = lax.axis_index("tp")
    grp_i = lax.axis_index("grp")
    core = lax.rem(tp_i, 2)
    chip = tp_i // 2
    other = 1 - core
    partner = {"tp": chip * 2 + other}

    def peer(dy):
        return lax.rem(chip + dy, chips)

    def peer_id(dy):
        return {"tp": peer(dy) * 2 + core}

    loads = [
        pltpu.make_async_copy(src, dst, w_sem.at[i])
        for i, (src, dst) in enumerate(
            [
                (x_hbm.at[:, 0], xg.at[:, tp_i]),
                (taps_hbm.at[:, 0], taps),
                (wkt_hbm, wkt),
                (wup_hbm, wup),
                (wdn_hbm, wdn),
                (wko_hbm, wko),
            ]
        )
    ]
    for load in loads:
        load.start()

    barrier = pltpu.get_barrier_semaphore()
    pl.semaphore_signal(barrier, inc=1, device_id=partner, device_id_type=MESH)
    for dy in range(1, chips):
        pl.semaphore_signal(barrier, inc=1, device_id=peer_id(dy), device_id_type=MESH)

    @pl.when(grp_i > 0)
    def _():
        pl.semaphore_signal(barrier, inc=1, device_id={"grp": grp_i - 1}, device_id_type=MESH)

    @pl.when(grp_i < grp_n - 1)
    def _():
        pl.semaphore_signal(barrier, inc=1, device_id={"grp": grp_i + 1}, device_id_type=MESH)

    neighbours = jnp.where(grp_i > 0, 1, 0) + jnp.where(grp_i < grp_n - 1, 1, 0)
    pl.semaphore_wait(barrier, chips + neighbours)

    def rows(ch):
        return pl.ds(ch * rc, rc)

    def own_rows(ch):
        turned = [xg[t, tp_i].T for t in chunk_tiles[ch]]
        return jnp.concatenate(turned, axis=0).astype(F32)

    def x_copy(t, dy):
        return pltpu.make_async_remote_copy(
            src_ref=x_hbm.at[t, 0],
            dst_ref=xg.at[t, tp_i],
            send_sem=x_ssem.at[t, dy],
            recv_sem=x_rsem.at[t, dy],
            device_id=peer_id(dy) if dy else partner,
            device_id_type=MESH,
        )

    def x_pass(t, dy):
        slot = lax.rem(chip - dy + chips, chips) * 2 + core
        return pltpu.make_async_remote_copy(
            src_ref=xg.at[t, slot],
            dst_ref=xg.at[t, slot],
            send_sem=xp_ssem.at[t, dy],
            recv_sem=xp_rsem.at[t, dy],
            device_id=partner,
            device_id_type=MESH,
        )

    def x_forward(ch):
        for t in chunk_tiles[ch]:
            for dy in range(1, chips):
                x_copy(t, dy).wait_recv()
                x_pass(t, dy).start()

    for t in order:
        for dy in list(range(1, chips)) + [0]:
            x_copy(t, dy).start()

    kv_cols = kvt.shape[1]

    def tap_product(ch):
        step = min(512, kv_cols)

        def body(j, carry):
            cols = pl.ds(pl.multiple_of(j * step, step), step)
            kvt[rows(ch), cols] = jnp.dot(
                tap_rows[rows(ch), :], wkt[:, cols], preferred_element_type=F32
            )
            return carry

        lax.fori_loop(0, kv_cols // step, body, 0)

    def up(ch):
        if ch == 0:
            loads[0].wait()
        for t in chunk_tiles[ch]:
            x_copy(t, 0).wait_recv()
            for dy in range(1, chips):
                x_pass(t, dy).wait_recv()
        depth = tp_n * chan
        gain = gain_ref[...].reshape(1, depth)
        bias = bias_ref[...].reshape(1, depth)
        for i, t in enumerate(chunk_tiles[ch]):
            values = xg[t].reshape(depth, tile).astype(F32)
            average = jnp.mean(values, axis=0, keepdims=True)
            centered = values - average
            variance = jnp.mean(centered * centered, axis=0, keepdims=True)
            standard = (centered * lax.rsqrt(variance + epsilon)).T
            normed[i * tile : (i + 1) * tile, :] = (standard * gain + bias).astype(BF16)
        if ch == 0:
            loads[3].wait()
        units = hidden.shape[1]
        step = 256 if units % 256 == 0 else units

        def body(j, carry):
            cols = pl.ds(pl.multiple_of(j * step, step), step) if step < units else slice(None)
            pre = jnp.dot(normed[...], wup[:, cols], preferred_element_type=F32) + bup_ref[cols].reshape(1, step)
            hidden[:, cols] = (0.5 * pre * (1.0 + lax.erf(pre * (0.5**0.5)))).astype(BF16)
            return carry

        lax.fori_loop(0, units // step, body, 0)

    def down(ch):
        if ch == 0:
            loads[4].wait()
        terms = jnp.dot(hidden[...], wdn[...], preferred_element_type=F32).astype(BF16)
        for t in range(tp_n):
            m_send[ch, t % 2, t // 2] = terms[:, t * chan : (t + 1) * chan]

    def l1(which, ch):
        send, r1 = (m_send, m_r1) if which == 0 else (k_send, k_r1)
        return pltpu.make_async_remote_copy(
            src_ref=send.at[ch, other],
            dst_ref=r1.at[ch],
            send_sem=l1_ssem.at[which, ch],
            recv_sem=l1_rsem.at[which, ch],
            device_id=partner,
            device_id_type=MESH,
        )

    def l2(which, ch, dy):
        s2, r2 = (m_s2, m_r2) if which == 0 else (k_s2, k_r2)
        return pltpu.make_async_remote_copy(
            src_ref=s2.at[ch, dy - 1],
            dst_ref=r2.at[ch, dy - 1],
            send_sem=l2_ssem.at[which, ch, dy - 1],
            recv_sem=l2_rsem.at[which, ch, dy - 1],
            device_id=peer_id(dy),
            device_id_type=MESH,
        )

    def level2(which, ch):
        send, r1, s2 = (m_send, m_r1, m_s2) if which == 0 else (k_send, k_r1, k_s2)
        l1(which, ch).wait_recv()
        for dy in range(1, chips):
            y = peer(dy)
            s2[ch, dy - 1] = (send[ch, core, y].astype(F32) + r1[ch, y].astype(F32)).astype(BF16)
            l2(which, ch, dy).start()

    def summed(which, ch):
        send, r1, r2 = (m_send, m_r1, m_r2) if which == 0 else (k_send, k_r1, k_r2)
        total = send[ch, core, chip].astype(F32) + r1[ch, chip].astype(F32)
        for dy in range(1, chips):
            l2(which, ch, dy).wait_recv()
            total = total + r2[ch, dy - 1].astype(F32)
        return total

    def project(ch):
        if ch == 0:
            loads[5].wait()
        encoded = (
            own_rows(ch) + summed(0, ch) + bdn_ref[...].reshape(1, chan)
        ).astype(BF16)
        for t in range(tp_n):
            start = t * KVH // tp_n * (2 * HD)
            cols = slice(start, start + width)
            k_send[ch, t % 2, t // 2] = (
                jnp.dot(encoded, wko[:, cols], preferred_element_type=F32) + kvt[rows(ch), cols]
            ).astype(BF16)

    def finish(ch):
        total = summed(1, ch)
        for h in range(width // (2 * HD)):
            key = total[:, 2 * h * HD : (2 * h + 1) * HD]
            square = jnp.mean(key * key, axis=-1, keepdims=True)
            key = (key * lax.rsqrt(square + epsilon) * kgain_ref[...]).astype(BF16)
            value = total[:, (2 * h + 1) * HD : (2 * h + 2) * HD]
            value = (value * (1.0 / VALUE_SCALE)).astype(BF16)
            for i, t in enumerate(chunk_tiles[ch]):
                part = slice(i * tile, (i + 1) * tile)
                kvg[t, grp_i, :, 2 * h * HD : (2 * h + 1) * HD] = key[part]
                kvg[t, grp_i, :, (2 * h + 1) * HD : (2 * h + 2) * HD] = value[part]

    def least(p):
        return jnp.maximum(REQ_G * p, total_tiles - REQ_G * MAXT * (grp_n - p))

    def most(p):
        return jnp.minimum(REQ_G * MAXT * (p + 1), total_tiles - REQ_G * (grp_n - 1 - p))

    def z_copy(t, way, k):
        block = grp_i - k if way == 0 else grp_i + k
        block = jnp.clip(block, 0, grp_n - 1)
        target = grp_i + 1 if way == 0 else grp_i - 1
        return pltpu.make_async_remote_copy(
            src_ref=kvg.at[t, block],
            dst_ref=kvg.at[t, block],
            send_sem=z_ssem.at[way, t, k],
            recv_sem=z_rsem.at[way, t, k],
            device_id={"grp": target},
            device_id_type=MESH,
        )

    def z_sends(t, way, k):
        if way == 0:
            tile_id = t * grp_n + grp_i - k
            return (grp_i - k >= 0) & (grp_i < grp_n - 1) & (tile_id >= least(grp_i + 1))
        tile_id = t * grp_n + grp_i + k
        return (grp_i + k <= grp_n - 1) & (grp_i > 0) & (tile_id < most(grp_i - 1))

    def z_gets(t, way, k):
        if way == 0:
            return (grp_i - k - 1 >= 0) & (t * grp_n + grp_i - k - 1 >= least(grp_i))
        return (grp_i + k + 1 <= grp_n - 1) & (t * grp_n + grp_i + k + 1 < most(grp_i))

    def z_start(t, k):
        for way in range(2):
            @pl.when(z_sends(t, way, k))
            def _(way=way):
                z_copy(t, way, k).start()

    def out_copy(t, block):
        return pltpu.make_async_copy(kvg.at[t, block], out_hbm.at[t, block], o_sem.at[t, block])

    def owned(t, block):
        tile_id = t * grp_n + block
        return (tile_id >= least(grp_i)) & (tile_id < most(grp_i))

    def z_hop(t, k):
        for way in range(2):
            @pl.when(z_gets(t, way, k))
            def _(way=way):
                z_copy(t, way, k).wait_recv()
            if k + 1 < grp_n - 1:
                @pl.when(z_sends(t, way, k + 1))
                def _(way=way):
                    z_copy(t, way, k + 1).start()

    loads[1].wait()
    for i, t in enumerate(order):
        tap_rows[i * tile : (i + 1) * tile, :] = taps[t].T
    loads[2].wait()
    ahead = min(2, nch)
    for ch in range(ahead):
        tap_product(ch)
        x_forward(ch)
    for step in range(nch + grp_n + 4):
        if step < nch:
            up(step)
        if 0 <= step - 1 < nch:
            level2(0, step - 1)
        if step < nch:
            down(step)
            l1(0, step).start()
        if ahead <= step + ahead < nch:
            x_forward(step + ahead)
        if ahead <= step + ahead < nch:
            tap_product(step + ahead)
        if 0 <= step - 2 < nch:
            project(step - 2)
            l1(1, step - 2).start()
            level2(1, step - 2)
        if 0 <= step - 3 < nch:
            finish(step - 3)
            for t in chunk_tiles[step - 3]:
                z_start(t, 0)
        for k in range(grp_n - 1):
            if 0 <= step - 4 - k < nch:
                for t in chunk_tiles[step - 4 - k]:
                    z_hop(t, k)

    for t in range(n_tiles):
        for block in range(grp_n):
            @pl.when(owned(t, block))
            def _(t=t, block=block):
                out_copy(t, block).start()
    for t in range(n_tiles):
        for dy in range(chips):
            x_copy(t, dy).wait_send()
        for dy in range(1, chips):
            x_pass(t, dy).wait_send()
        for k in range(grp_n - 1):
            for way in range(2):
                @pl.when(z_sends(t, way, k))
                def _(t=t, way=way, k=k):
                    z_copy(t, way, k).wait_send()
    for ch in range(nch):
        for which in range(2):
            l1(which, ch).wait_send()
            for dy in range(1, chips):
                l2(which, ch, dy).wait_send()
    for t in range(n_tiles):
        for block in range(grp_n):
            @pl.when(owned(t, block))
            def _(t=t, block=block):
                out_copy(t, block).wait()


def attend_kernel(
    tiles_ref, owner_ref, text_ref, q_ref, qgain_ref, kv_hbm, out_ref, kbuf, vbuf, vext, sem
):
    _, grp_n, _, width = kv_hbm.shape
    kv_heads = width // (2 * HD)
    requests, _, window, _ = kbuf.shape
    tile = window // MAXT
    head, rb = pl.program_id(0), pl.program_id(1)
    group = lax.axis_index("grp")
    offset = jnp.int32(0)
    tiles = [jnp.int32(0)] * requests
    texts = [jnp.int32(0)] * requests
    seen = jnp.int32(0)
    for r in range(owner_ref.shape[0]):
        own = owner_ref[r] == group
        offset = offset + jnp.where(owner_ref[r] < group, tiles_ref[r], 0)
        for i in range(requests):
            here = own & (seen == i)
            tiles[i] = jnp.where(here, tiles_ref[r], tiles[i])
            texts[i] = jnp.where(here, text_ref[r], texts[i])
        seen = seen + own.astype(jnp.int32)

    def copies(i, h, j):
        first = jnp.int32(0) if i == 0 else tiles[0]
        index = offset + first + jnp.where(j < tiles[i], j, 0)
        src = kv_hbm.at[index // grp_n, lax.rem(index, grp_n)]
        dst = pl.ds(j * tile, tile)
        return (
            pltpu.make_async_copy(
                src.at[:, pl.ds(2 * h * HD, HD)], kbuf.at[i, h, dst], sem.at[0, i, h, j]
            ),
            pltpu.make_async_copy(
                src.at[:, pl.ds((2 * h + 1) * HD, HD)], vbuf.at[i, h, dst], sem.at[1, i, h, j]
            ),
        )

    @pl.when((head == 0) & (rb == 0))
    def _():
        for h in range(kv_heads):
            for i in range(requests):
                for j in range(MAXT):
                    for c in copies(i, h, j):
                        c.start()
        for h in range(kv_heads):
            for i in range(requests):
                for j in range(MAXT):
                    for c in copies(i, h, j):
                        c.wait()
                    rows = slice(j * tile, (j + 1) * tile)
                    live = j < tiles[i]
                    vext[i, h, rows, :HD] = jnp.where(live, vbuf[i, h, rows, :], 0).astype(BF16)
                    vext[i, h, rows, HD:] = jnp.where(live, jnp.ones((tile, HD), F32), 0.0).astype(BF16)

    block = q_ref.shape[0]
    per_head = q_ref.shape[1] // HD
    factor = qgain_ref[...] * (LOG2E / float(HD) ** 0.5)
    out_ref[...] = jnp.zeros_like(out_ref)
    row = lax.broadcasted_iota(jnp.int32, (block, 1), 0) + rb * block
    for i in range(requests):
        low = jnp.int32(0) if i == 0 else texts[0]
        high = low + texts[i]

        @pl.when((low < (rb + 1) * block) & (high > rb * block))
        def _():
            live = (row >= low) & (row < high)
            keys = kbuf[i, head]
            values = vext[i, head]
            for g in range(per_head):
                cols = slice(g * HD, (g + 1) * HD)
                query = q_ref[:, cols].astype(F32)
                square = jnp.mean(query * query, axis=-1, keepdims=True)
                query = (query * lax.rsqrt(square + epsilon) * factor).astype(BF16)
                scores = lax.dot_general(
                    query, keys, (((1,), (1,)), ((), ())), preferred_element_type=F32
                )
                weights = jnp.exp2(scores).astype(BF16)
                result = jnp.dot(weights, values, preferred_element_type=F32)
                shared = result[:, :HD] * (VALUE_SCALE / result[:, HD:])
                out_ref[:, cols] += jnp.where(live, shared, 0.0).astype(BF16)


def local(
    x_in,
    taps,
    ln_gain,
    ln_bias,
    w_up,
    b_up,
    w_down,
    b_down,
    kv_w_out,
    kv_w_taps,
    k_gain,
    q_gain,
    queries,
    tiles_per_request,
    owner,
    text_per_request,
):
    grp_n = lax.axis_size("grp")
    tp_n = lax.axis_size("tp")
    chips = tp_n // 2
    tiles_local, _, tile, chan = x_in.shape
    n = tiles_local * tile
    nch = tiles_local
    rc = n // nch
    depth, units = w_up.shape
    tap_share, kv_cols = kv_w_taps.shape
    width = max(1, KVH // tp_n) * 2 * HD
    any_spec = pl.BlockSpec(memory_space=pl.ANY)
    vmem_spec = pl.BlockSpec(memory_space=pltpu.VMEM)
    dma = pltpu.SemaphoreType.DMA
    gathered = pl.pallas_call(
        functools.partial(front_kernel, (tp_n, grp_n, nch, rc, chan, width)),
        name="front",
        out_shape=jax.ShapeDtypeStruct((tiles_local, grp_n, tile, width), BF16),
        in_specs=[
            any_spec,
            any_spec,
            vmem_spec,
            vmem_spec,
            any_spec,
            vmem_spec,
            any_spec,
            vmem_spec,
            any_spec,
            any_spec,
            vmem_spec,
        ],
        out_specs=any_spec,
        scratch_shapes=[
            pltpu.VMEM((tiles_local, tp_n, chan, tile), BF16),
            pltpu.VMEM((rc, depth), BF16),
            pltpu.VMEM((rc, units), BF16),
            pltpu.VMEM((tiles_local, tap_share, tile), BF16),
            pltpu.VMEM((n, tap_share), BF16),
            pltpu.VMEM(w_up.shape, BF16),
            pltpu.VMEM(w_down.shape, BF16),
            pltpu.VMEM(kv_w_out.shape, BF16),
            pltpu.VMEM(kv_w_taps.shape, BF16),
            pltpu.VMEM((n, kv_cols), F32),
            pltpu.VMEM((nch, 2, chips, rc, chan), BF16),
            pltpu.VMEM((nch, chips, rc, chan), BF16),
            pltpu.VMEM((nch, chips - 1, rc, chan), BF16),
            pltpu.VMEM((nch, chips - 1, rc, chan), BF16),
            pltpu.VMEM((nch, 2, chips, rc, width), BF16),
            pltpu.VMEM((nch, chips, rc, width), BF16),
            pltpu.VMEM((nch, chips - 1, rc, width), BF16),
            pltpu.VMEM((nch, chips - 1, rc, width), BF16),
            pltpu.VMEM((tiles_local, grp_n, tile, width), BF16),
            dma((6,)),
            dma((tiles_local, chips)),
            dma((tiles_local, chips)),
            dma((tiles_local, chips)),
            dma((tiles_local, chips)),
            dma((2, nch)),
            dma((2, nch)),
            dma((2, nch, chips - 1)),
            dma((2, nch, chips - 1)),
            dma((2, tiles_local, grp_n - 1)),
            dma((2, tiles_local, grp_n - 1)),
            dma((tiles_local, grp_n)),
        ],
        compiler_params=pltpu.CompilerParams(
            collective_id=0, has_side_effects=True, vmem_limit_bytes=VMEM_BYTES
        ),
    )(
        jnp.swapaxes(x_in, 2, 3),
        jnp.swapaxes(taps, 2, 3),
        ln_gain,
        ln_bias,
        w_up,
        b_up,
        w_down,
        b_down,
        kv_w_out,
        kv_w_taps,
        k_gain.reshape(1, HD),
    )
    text_rows, query_width = queries.shape
    heads = query_width // HD
    kv_heads = width // (2 * HD)
    block = 128 if text_rows % 128 == 0 else text_rows
    per_head = heads // kv_heads * HD
    spec = pl.BlockSpec((block, per_head), lambda h, r, *_: (r, h))
    return pl.pallas_call(
        attend_kernel,
        name="attend",
        out_shape=jax.ShapeDtypeStruct(queries.shape, BF16),
        grid_spec=pltpu.PrefetchScalarGridSpec(
            num_scalar_prefetch=3,
            grid=(kv_heads, text_rows // block),
            in_specs=[spec, pl.BlockSpec((1, HD), lambda h, r, *_: (0, 0)), any_spec],
            out_specs=spec,
            scratch_shapes=[
                pltpu.VMEM((REQ_G, kv_heads, MAXT * tile, HD), BF16),
                pltpu.VMEM((REQ_G, kv_heads, MAXT * tile, HD), BF16),
                pltpu.VMEM((REQ_G, kv_heads, MAXT * tile, 2 * HD), BF16),
                dma((2, REQ_G, kv_heads, MAXT)),
            ],
        ),
        compiler_params=pltpu.CompilerParams(vmem_limit_bytes=VMEM_BYTES),
    )(tiles_per_request, owner, text_per_request, queries, q_gain.reshape(1, HD), gathered)


def solution(mesh):
    in_specs = (
        P(None, ("rep", "grp"), None, "tp"),
        P(None, ("rep", "grp"), None, "tp"),
        P(),
        P(),
        P(None, "tp"),
        P("tp"),
        P("tp", None),
        P("tp"),
        P("tp", None),
        P("tp", None),
        P(),
        P(),
        P(("rep", "grp"), "tp"),
        P("rep"),
        P("rep"),
        P("rep"),
    )
    out_specs = P(("rep", "grp"), "tp")
    return jax.shard_map(local, mesh=mesh, in_specs=in_specs, out_specs=out_specs, check_vma=False)
```
